32 devices in a mesh: fsdp: 8 (over z, y), seq: 4 (over x, core).
Axes of the slice: x: 2, y: 2, z: 4, core: 2. Of those that a mesh axis runs over, the one named last changes fastest.
Arguments:
- frames_in: bfloat16 [16, 1536, 1280], P('fsdp', 'seq'), may hold values from -6 to 6
- teacher: bfloat16 [16, 1536, 1280], P('fsdp', 'seq'), may hold values from -6 to 6
- lengths: int32 [16], replicated, may hold values from 384 to 1536, as said below
- norm1_gain: bfloat16 [1280], P('fsdp'), may hold values from 0.25 to 1.75
- norm1_bias: bfloat16 [1280], P('fsdp'), may hold values from -1.75 to 1.75
- w_qkv: bfloat16 [1280, 3840], P('fsdp'), may hold values from -0.15625 to 0.15625
- query_bias: bfloat16 [1280], P('fsdp'), may hold values from -1.75 to 1.75
- value_bias: bfloat16 [1280], P('fsdp'), may hold values from -1.75 to 1.75
- w_attn_out: bfloat16 [1280, 1280], P('fsdp'), may hold values from -0.875 to 0.875
- attn_out_bias: bfloat16 [1280], P('fsdp'), may hold values from -1.75 to 1.75
- norm2_gain: bfloat16 [1280], P('fsdp'), may hold values from 0.25 to 1.75
- norm2_bias: bfloat16 [1280], P('fsdp'), may hold values from -1.75 to 1.75
- w_up: bfloat16 [1280, 5120], P('fsdp'), may hold values from -0.15625 to 0.15625
- up_bias: bfloat16 [5120], P('fsdp'), may hold values from -1.75 to 1.75
- w_down: bfloat16 [5120, 1280], P('fsdp'), may hold values from -0.125 to 0.125
- down_bias: bfloat16 [1280], P('fsdp'), may hold values from -1.75 to 1.75
Outputs:
- frames_out: bfloat16 [16, 1536, 1280], P('fsdp', 'seq')
- clip_loss: float32 [16], P('fsdp')
- grad_in: float32 [16, 1536, 1280], P('fsdp', 'seq')
- grad_norm1_gain: float32 [1280], P('fsdp')
- grad_norm1_bias: float32 [1280], P('fsdp')
- grad_w_qkv: float32 [1280, 3840], P('fsdp')
- grad_query_bias: float32 [1280], P('fsdp')
- grad_value_bias: float32 [1280], P('fsdp')
- grad_w_attn_out: float32 [1280, 1280], P('fsdp')
- grad_attn_out_bias: float32 [1280], P('fsdp')
- grad_norm2_gain: float32 [1280], P('fsdp')
- grad_norm2_bias: float32 [1280], P('fsdp')
- grad_w_up: float32 [1280, 5120], P('fsdp')
- grad_up_bias: float32 [5120], P('fsdp')
- grad_w_down: float32 [5120, 1280], P('fsdp')
- grad_down_bias: float32 [1280], P('fsdp')
The draws below stay inside these ranges and needn't reach their ends.
Inputs may be any that keep to these rules, and one draw needn't show every extreme that they name: `lengths`: a clip's valid frames are its first ones; in every draw some clip has all 1536 frames valid.
All inputs are finite; a program needn't handle non-finite values.
Results may differ from the reference program's by a relative error of at most 0.0095.
Values may be sent and summed in bfloat16 or wider, within the bound.
A program may use at most 256 MiB of HBM per device.

```python
import math
import jax
import jax.numpy as jnp
from jax import lax

D = 1280
HEADS = 16
FF = 5120
HEAD = 80
LENGTH = 1536
CLIPS = 16


def draw_lengths(key, part):
    first, second = jax.random.split(jax.random.fold_in(key, 7))
    drawn = jax.random.randint(first, (CLIPS,), LENGTH // 4, LENGTH + 1)
    spot = jax.random.randint(second, (), 0, CLIPS)
    return jnp.where(jnp.arange(CLIPS) == spot, LENGTH, drawn).astype(jnp.int32)


def shard_levels(own_key, dims, cuts, low, top_value):
    level = 1.0
    for axis_at, blocks in cuts:
        steps = jax.random.uniform(jax.random.fold_in(jax.random.fold_in(own_key, 6), axis_at), (blocks,), jnp.float32, low / len(cuts), top_value / len(cuts))
        level = level * jnp.repeat(jnp.exp(steps), dims[axis_at] // blocks).reshape((-1,) + (1,) * (len(dims) - 1 - axis_at))
    return level


def normal_values(stream_key, dims, scale, bound, cuts=(), kind=jnp.bfloat16):
    entries = scale * jax.random.normal(stream_key, dims, jnp.float32)
    if cuts:
        entries = entries * shard_levels(stream_key, dims, cuts, -0.22, 0.18)
    return jnp.clip(entries, -bound, bound).astype(kind)


def setup_inputs(seed: int = 0) -> dict:
    arg_keys = jax.random.split(jax.random.key(seed), 17)
    frames_in = normal_values(arg_keys[0], (CLIPS, LENGTH, D), 1.0, 6.0, ((0, 8), (1, 4)))
    teacher = normal_values(arg_keys[1], (CLIPS, LENGTH, D), 1.0, 6.0, ((0, 8), (1, 4)))
    lengths = draw_lengths(jax.random.fold_in(arg_keys[16], 71), 0)
    norm1_gain = jnp.clip(1.0 + 0.15 * jax.random.normal(arg_keys[3], (D,), jnp.float32), 0.25, 1.75).astype(jnp.bfloat16)
    norm1_bias = normal_values(arg_keys[4], (D,), 0.3, 1.75, ((0, 8),))
    w_qkv = normal_values(arg_keys[5], (D, 3 * D), D ** -0.5, 0.15625, ((0, 8),))
    query_bias = normal_values(arg_keys[6], (D,), 0.3, 1.75, ((0, 8),))
    value_bias = normal_values(arg_keys[7], (D,), 0.3, 1.75, ((0, 8),))
    w_attn_out = normal_values(arg_keys[8], (D, D), (D // 24) ** -0.5, 0.875, ((0, 8),))
    attn_out_bias = normal_values(arg_keys[9], (D,), 0.3, 1.75, ((0, 8),))
    norm2_gain = jnp.clip(1.0 + 0.15 * jax.random.normal(arg_keys[10], (D,), jnp.float32), 0.25, 1.75).astype(jnp.bfloat16)
    norm2_bias = normal_values(arg_keys[11], (D,), 0.3, 1.75, ((0, 8),))
    w_up = normal_values(arg_keys[12], (D, FF), D ** -0.5, 0.15625, ((0, 8),))
    up_bias = normal_values(arg_keys[13], (FF,), 0.3, 1.75, ((0, 8),))
    w_down = normal_values(arg_keys[14], (FF, D), (FF // 2) ** -0.5, 0.125, ((0, 8),))
    down_bias = normal_values(arg_keys[15], (D,), 0.3, 1.75, ((0, 8),))
    return {"frames_in": frames_in, "teacher": teacher, "lengths": lengths, "norm1_gain": norm1_gain, "norm1_bias": norm1_bias, "w_qkv": w_qkv, "query_bias": query_bias, "value_bias": value_bias, "w_attn_out": w_attn_out, "attn_out_bias": attn_out_bias, "norm2_gain": norm2_gain, "norm2_bias": norm2_bias, "w_up": w_up, "up_bias": up_bias, "w_down": w_down, "down_bias": down_bias}


@jax.custom_vjp
def low(v):
    return lax.optimization_barrier(v.astype(jnp.bfloat16)).astype(jnp.float32)

@jax.custom_vjp
def low_back(v):
    return v

def low_keep(v):
    return (low(v), None)

def low_pass(kept, grad):
    return (grad,)

def back_keep(v):
    return (v, None)

def back_low(kept, grad):
    return (low(grad),)
low.defvjp(low_keep, low_pass)
low_back.defvjp(back_keep, back_low)

def layer_norm(v, gain, bias):
    mean = lax.optimization_barrier(jnp.mean(v, axis=-1, keepdims=True))
    cent = v - mean
    var = lax.optimization_barrier(jnp.mean(cent * cent, axis=-1, keepdims=True))
    return cent * lax.rsqrt(var + 1e-05) * gain + bias

def matmul(a, b):
    return jnp.dot(a, b, precision=lax.Precision.HIGHEST, preferred_element_type=jnp.float32)

def clip_layer(params, clip_in, clip_teacher, length, count):
    gain1, bias1, wqkv, qbias, vbias, wout, obias, gain2, bias2, wup, ubias, wdown, dbias = params
    hidden1 = low(layer_norm(clip_in, gain1, bias1))
    qkv = matmul(hidden1, wqkv)
    query = low(low_back(qkv[:, :D] + qbias)).reshape(LENGTH, HEADS, HEAD)
    keyed = low(low_back(qkv[:, D:2 * D])).reshape(LENGTH, HEADS, HEAD)
    valued = low(low_back(qkv[:, 2 * D:] + vbias)).reshape(LENGTH, HEADS, HEAD)
    valid = jnp.arange(LENGTH, dtype=jnp.int32) < length
    scores = jnp.einsum('qhd,khd->hqk', query, keyed, precision=lax.Precision.HIGHEST) * (1.0 / math.sqrt(HEAD))
    scores = low_back(scores)
    scores = jnp.where(valid[None, None, :], scores, -1e+30)
    top = lax.optimization_barrier(jnp.max(scores, axis=-1, keepdims=True))
    expo = jnp.exp(scores - top)
    probs = low(expo / lax.optimization_barrier(jnp.sum(expo, axis=-1, keepdims=True)))
    context = jnp.einsum('hqk,khd->qhd', probs, valued, precision=lax.Precision.HIGHEST)
    context = low(low_back(context)).reshape(LENGTH, D)
    attn = low_back(matmul(context, wout) + obias)
    middle = clip_in + attn
    hidden2 = low(layer_norm(middle, gain2, bias2))
    upper = low_back(matmul(hidden2, wup) + ubias)
    active = low(jax.nn.gelu(upper, approximate=False))
    branch = low_back(matmul(active, wdown) + dbias)
    result = middle + branch
    diff = result - clip_teacher
    squares = jnp.sum(jnp.where(valid[:, None], diff * diff, 0.0))
    return (result, squares / (2.0 * D * count))

def reference(frames_in, teacher, lengths, norm1_gain, norm1_bias, w_qkv, query_bias, value_bias, w_attn_out, attn_out_bias, norm2_gain, norm2_bias, w_up, up_bias, w_down, down_bias):
    params = tuple((p.astype(jnp.float32) for p in (norm1_gain, norm1_bias, w_qkv, query_bias, value_bias, w_attn_out, attn_out_bias, norm2_gain, norm2_bias, w_up, up_bias, w_down, down_bias)))
    count = jnp.sum(lengths).astype(jnp.float32)
    scaling = jnp.asarray(float(D * CLIPS * LENGTH), jnp.float32)

    def step(totals, item):
        clip_in, clip_teacher, length = item

        def forward(prm, state):
            return clip_layer(prm, state, clip_teacher.astype(jnp.float32), length, count)
        (result, loss), backward = jax.vjp(forward, params, clip_in.astype(jnp.float32))
        grad_params, grad_state = backward((jnp.zeros_like(result), scaling))
        totals = tuple((a + g for a, g in zip(totals, grad_params)))
        return (totals, (result.astype(jnp.bfloat16), loss, grad_state))
    start = tuple((jnp.zeros_like(p) for p in params))
    totals, (outs, losses, grads_in) = lax.scan(step, start, (frames_in, teacher, lengths))
    return (outs, losses, grads_in, totals[0], totals[1], totals[2], totals[3], totals[4], totals[5], totals[6], totals[7], totals[8], totals[9], totals[10], totals[11], totals[12])
```

```python
import functools
import math

import jax
import jax.numpy as jnp
from jax import lax
from jax.experimental import pallas as pl
from jax.experimental.pallas import tpu as pltpu
from jax.sharding import PartitionSpec as P

HEADS = 16
LANES = 128
LOG2E = 1.0 / math.log(2.0)
single = jnp.float32
half = jnp.bfloat16


def layer_norm(v, gain, bias):
    mean = jnp.mean(v, axis=-1, keepdims=True)
    cent = v - mean
    var = jnp.mean(cent * cent, axis=-1, keepdims=True)
    return cent * lax.rsqrt(var + 1e-05) * gain + bias


def flip(tensor, bits, axis="seq"):
    return lax.ppermute(
        tensor, axis, [(i, i ^ bits) for i in range(lax.axis_size(axis))]
    )


def gather_all(piece):
    groups = lax.axis_size("seq")
    blocks = {0: piece}
    bits = groups // 2
    while bits:
        for r in sorted(blocks):
            blocks[r | bits] = flip(blocks[r], bits)
        bits //= 2
    return [blocks[r] for r in range(groups)]


def scatter_sum(partial):
    groups = lax.axis_size("seq")
    n = partial.shape[0] // groups
    terms = {r: partial[r * n : (r + 1) * n] for r in range(groups)}
    bits = 1
    while bits < groups:
        for r in reversed(range(0, groups, 2 * bits)):
            terms[r] = terms[r].astype(single) + flip(terms[r | bits].astype(half), bits).astype(single)
        bits *= 2
    return terms[0]


def swap(parts):
    return [parts[0]] + [flip(parts[r], r) for r in range(1, len(parts))]


def pad_lanes(tensor, tail):
    return jnp.concatenate([tensor, tail], axis=1)


def unit_tail(rows, width):
    lane = lax.broadcasted_iota(jnp.int32, (rows, width), 1)
    return jnp.where(lane == 0, 1.0, 0.0).astype(half)


def attend_kernel(heads, dim, block, scale, qkv_ref, mask_ref, ctx_ref, lse_ref, keys, values):
    seq = qkv_ref.shape[0]
    span = heads * dim
    rest = LANES - dim
    rate = scale * LOG2E
    for j in range(heads):
        keys[j] = pad_lanes(
            qkv_ref[:, span + j * dim : span + (j + 1) * dim], mask_ref[...]
        )
        values[j] = pad_lanes(
            qkv_ref[:, 2 * span + j * dim : 2 * span + (j + 1) * dim], unit_tail(seq, rest)
        )

    def one_block(i, carry):
        rows = pl.ds(pl.multiple_of(i * block, block), block)
        ones = unit_tail(block, rest)
        contexts, sums = [], []
        for j in range(heads):
            query = pad_lanes(qkv_ref[rows, j * dim : (j + 1) * dim], ones)
            scores = lax.dot_general(
                query, keys[j], (((1,), (1,)), ((), ())), preferred_element_type=single
            )
            top = jnp.max(scores, axis=-1, keepdims=True) * rate
            probs = jnp.exp2(scores * rate - top).astype(half)
            mixed = jnp.dot(probs, values[j], preferred_element_type=single)
            total = mixed[:, dim : dim + 1]
            contexts.append((mixed[:, :dim] / total).astype(half))
            sums.append(top + jnp.log(total) * LOG2E)
        ctx_ref[rows, :] = jnp.concatenate(contexts, axis=1)
        lse_ref[rows, :] = jnp.concatenate(sums, axis=1)
        return carry

    lax.fori_loop(0, seq // block, one_block, 0)


def attend_back_kernel(
    heads, dim, block, scale,
    qkv_ref, mask_ref, grad_ref, lse_ref, out_ref, keys, values, gkeys, gvalues, gquery,
):
    seq = qkv_ref.shape[0]
    span = heads * dim
    rest = LANES - dim
    rate = scale * LOG2E
    for j in range(heads):
        keys[j] = pad_lanes(
            qkv_ref[:, span + j * dim : span + (j + 1) * dim], mask_ref[...]
        )
        values[j] = pad_lanes(
            qkv_ref[:, 2 * span + j * dim : 2 * span + (j + 1) * dim],
            jnp.zeros((seq, rest), half),
        )
    gkeys[...] = jnp.zeros_like(gkeys)
    gvalues[...] = jnp.zeros_like(gvalues)

    def one_block(i, carry):
        rows = pl.ds(pl.multiple_of(i * block, block), block)
        ones = unit_tail(block, rest)
        none = jnp.zeros((block, rest), half)
        pieces = []
        for j in range(heads):
            query = pad_lanes(qkv_ref[rows, j * dim : (j + 1) * dim], ones)
            grad = pad_lanes(grad_ref[rows, j * dim : (j + 1) * dim], none)
            scores = lax.dot_general(
                query, keys[j], (((1,), (1,)), ((), ())), preferred_element_type=single
            )
            probs = jnp.exp2(scores * rate - lse_ref[rows, j : j + 1])
            dprobs = lax.dot_general(
                grad, values[j], (((1,), (1,)), ((), ())), preferred_element_type=single
            )
            inner = jnp.sum(probs * dprobs, axis=-1, keepdims=True)
            dscores = (probs * (dprobs - inner)).astype(half)
            pieces.append(
                (jnp.dot(dscores, keys[j], preferred_element_type=single)[:, :dim] * scale).astype(half)
            )
            gkeys[j] += jnp.dot(query.T, dscores, preferred_element_type=single)
            gvalues[j] += jnp.dot(grad.T, probs.astype(half), preferred_element_type=single)
        gquery[rows, :] = jnp.concatenate(pieces, axis=1)
        return carry

    lax.fori_loop(0, seq // block, one_block, 0)

    def put(i, carry):
        rows = pl.ds(pl.multiple_of(i * block, block), block)
        pieces = [gquery[rows, :]]
        for j in range(heads):
            pieces.append((gkeys[j, :, rows].T[:, :dim] * scale).astype(half))
        for j in range(heads):
            pieces.append(gvalues[j, :, rows].T[:, :dim].astype(half))
        out_ref[rows, :] = jnp.concatenate(pieces, axis=1)
        return carry

    lax.fori_loop(0, seq // block, put, 0)


def attend(qkv, mask, heads, dim, scale):
    seq = qkv.shape[0]
    block = 256
    return pl.pallas_call(
        functools.partial(attend_kernel, heads, dim, block, scale),
        out_shape=(
            jax.ShapeDtypeStruct((seq, heads * dim), half),
            jax.ShapeDtypeStruct((seq, heads), single),
        ),
        scratch_shapes=[
            pltpu.VMEM((heads, seq, LANES), half),
            pltpu.VMEM((heads, seq, LANES), half),
        ],
        compiler_params=pltpu.CompilerParams(vmem_limit_bytes=48 << 20),
        cost_estimate=pl.CostEstimate(
            flops=4 * heads * seq * seq * 256, bytes_accessed=qkv.size * 3, transcendentals=heads * seq * seq
        ),
        name="attend",
    )(qkv, mask)


def attend_back(qkv, mask, grad, lse, heads, dim, scale):
    seq = qkv.shape[0]
    block = 256
    return pl.pallas_call(
        functools.partial(attend_back_kernel, heads, dim, block, scale),
        out_shape=jax.ShapeDtypeStruct(qkv.shape, half),
        scratch_shapes=[
            pltpu.VMEM((heads, seq, LANES), half),
            pltpu.VMEM((heads, seq, LANES), half),
            pltpu.VMEM((heads, LANES, seq), single),
            pltpu.VMEM((heads, LANES, seq), single),
            pltpu.VMEM((seq, heads * dim), half),
        ],
        compiler_params=pltpu.CompilerParams(vmem_limit_bytes=56 << 20),
        cost_estimate=pl.CostEstimate(
            flops=10 * heads * seq * seq * 256, bytes_accessed=qkv.size * 5, transcendentals=heads * seq * seq
        ),
        name="attend_back",
    )(qkv, mask, grad, lse)


def local(
    frames_in, teacher, lengths, norm1_gain, norm1_bias, w_qkv, query_bias, value_bias,
    w_attn_out, attn_out_bias, norm2_gain, norm2_bias, w_up, up_bias, w_down, down_bias,
):
    clips, frames, width = frames_in.shape
    groups = lax.axis_size("seq")
    owners = lax.axis_size("fsdp")
    me = lax.axis_index("seq")
    own = lax.axis_index("fsdp")
    seq_len = frames * groups
    dim = width // HEADS
    heads = HEADS // groups
    span = heads * dim
    depth = w_qkv.shape[0]
    units = w_down.shape[0]
    part = units // groups
    scale = 1.0 / math.sqrt(dim)

    def dot(a, b):
        return jnp.dot(a, b, preferred_element_type=single)

    def dot_t(a, b):
        return lax.dot_general(a, b, (((1,), (1,)), ((), ())), preferred_element_type=single)

    def t_dot(a, b):
        return lax.dot_general(a, b, (((0,), (0,)), ((), ())), preferred_element_type=single)

    def columns(array, start, size):
        return lax.dynamic_slice_in_dim(array, start, size, 1)

    states = [gather_all(frames_in[c]) for c in range(clips)]

    first = jnp.concatenate(
        [columns(w_qkv, k * width + me * span, span) for k in range(3)]
        + [columns(w_attn_out, me * span, span)],
        axis=1,
    )
    first = lax.all_gather(first, "fsdp", axis=0, tiled=True)
    ff = owners * part
    wup = jnp.concatenate([columns(w_up, f * units + me * part, part) for f in range(owners)], axis=1)
    wdown = lax.dynamic_slice_in_dim(w_down, me * part, part, 0)
    if part == depth:
        second = lax.all_gather(jnp.concatenate([wup, wdown], axis=1), "fsdp", axis=0, tiled=True)
        wup, wdown = second[:, :ff], second[:, ff:]
    else:
        wup = lax.all_gather(wup, "fsdp", axis=0, tiled=True)
        wdown = lax.all_gather(wdown, "fsdp", axis=0, tiled=True)
    wqkv = first[:, : 3 * span]

    packed = jnp.concatenate(
        [norm1_gain, norm1_bias, query_bias, value_bias, attn_out_bias, norm2_gain, norm2_bias,
         down_bias, up_bias]
    )[None]
    bits = 1
    while bits < owners:
        packed = jnp.concatenate([packed, flip(packed, bits, "fsdp")], axis=0)
        bits *= 2
    vectors = jnp.take(packed, own ^ jnp.arange(owners), axis=0).astype(single)

    def vector(k):
        return vectors[:, k * depth : (k + 1) * depth].reshape(1, width)

    gain1, bias1, qbias, vbias, obias, gain2, bias2, dbias = (vector(k) for k in range(8))
    ubias = lax.dynamic_slice_in_dim(vectors, 8 * depth + me * part, part, 1).reshape(1, ff)
    qkv_bias = jnp.concatenate(
        [columns(qbias, me * span, span), jnp.zeros((1, span), single), columns(vbias, me * span, span)],
        axis=1,
    )

    quarters = jnp.stack(gather_all(first[:, 3 * span :]))
    wout = jnp.concatenate(
        [lax.dynamic_index_in_dim(quarters, me ^ g, 0, keepdims=False) for g in range(groups)], axis=1
    )
    wout = jnp.concatenate(
        [lax.dynamic_slice_in_dim(wout, (me ^ r) * span, span, 0) for r in range(groups)], axis=0
    )

    mine = lax.dynamic_slice_in_dim(lengths, own * clips, clips)
    order = (me ^ jnp.arange(groups, dtype=jnp.int32))[:, None] * frames + jnp.arange(
        frames, dtype=jnp.int32
    )
    order = order.reshape(seq_len)
    count = jnp.sum(lengths).astype(single)
    lane0 = (jnp.arange(LANES - dim) == 0)[None, :]
    masks = [
        jnp.where((order >= mine[c])[:, None] & lane0, -1e30, 0.0).astype(half) for c in range(clips)
    ]
    row_valid = [(order[:frames] < mine[c]).astype(single)[:, None] for c in range(clips)]

    full1, qkvs, sums, contexts, middles, full2 = [], [], [], [], [], []
    for c in range(clips):
        state = jnp.concatenate(states[c], axis=0).astype(single)
        hidden = layer_norm(state, gain1, bias1).astype(half)
        qkv = (dot(hidden, wqkv) + qkv_bias).astype(half)
        context, lse = attend(qkv, masks[c], heads, dim, scale)
        full1.append(hidden)
        qkvs.append(qkv)
        sums.append(lse)
        context = swap([context[r * frames : (r + 1) * frames] for r in range(groups)])
        contexts.append(jnp.concatenate(context, axis=1))
    for c in range(clips):
        middle = frames_in[c].astype(single) + dot(contexts[c], wout) + obias
        hidden = layer_norm(middle, gain2, bias2).astype(half)
        middles.append(middle)
        full2.append(jnp.concatenate(gather_all(hidden), axis=0))
    actives, slopes, branches = [], [], []
    for c in range(clips):
        upper = dot(full2[c], wup) + ubias
        cdf = 0.5 * (1.0 + lax.erf(upper * math.sqrt(0.5)))
        actives.append((upper * cdf).astype(half))
        slopes.append(
            (cdf + upper * (jnp.exp(-0.5 * upper * upper) * (1.0 / math.sqrt(2.0 * math.pi)))).astype(half)
        )
        branches.append(scatter_sum(dot(actives[c], wdown).astype(half)))
    outs, losses, grad_outs, fulls = [], [], [], []
    for c in range(clips):
        result = middles[c] + branches[c] + dbias
        outs.append(result.astype(half))
        diff = result - teacher[c].astype(single)
        masked = diff * row_valid[c]
        losses.append(jnp.sum(masked * diff) / (2.0 * width * count))
        grad_out = masked * (float(lengths.shape[0] * seq_len) / count)
        grad_outs.append(grad_out)
        fulls.append(jnp.concatenate(gather_all(grad_out.astype(half)), axis=0))
    frames_out = jnp.stack(outs)

    def owned(grad):
        return lax.psum_scatter(grad.astype(half), "fsdp", scatter_dimension=0, tiled=True)

    grad_wdown = owned(sum(t_dot(actives[c], fulls[c]) for c in range(clips)))
    grad_dbias = sum(jnp.sum(g.astype(half).astype(single), axis=0) for g in grad_outs)
    grad_uppers = [
        (dot_t(fulls[c], wdown) * slopes[c].astype(single)).astype(half) for c in range(clips)
    ]
    grad_hidden2 = [scatter_sum(dot_t(grad_uppers[c], wup).astype(half)) for c in range(clips)]
    grad_wup = owned(sum(t_dot(full2[c], grad_uppers[c]) for c in range(clips)))
    grad_ubias = sum(jnp.sum(g.astype(single), axis=0) for g in grad_uppers)

    def norm_back(v, gain, bias, grad):
        _, back = jax.vjp(layer_norm, v, gain, bias)
        return back(grad)

    grad_gain2 = grad_bias2 = 0.0
    grad_middles, grad_branches, grad_heads = [], [], []
    for c in range(clips):
        gm, gg, gb = norm_back(middles[c], gain2, bias2, grad_hidden2[c])
        grad_gain2 += gg
        grad_bias2 += gb
        grad_middles.append(grad_outs[c] + gm)
        branch = grad_middles[c].astype(half)
        grad_branches.append(branch)
        grad_context = dot_t(branch, wout).astype(half)
        grad_context = swap([grad_context[:, r * span : (r + 1) * span] for r in range(groups)])
        grad_heads.append(jnp.concatenate(grad_context, axis=0))
    grad_obias = sum(jnp.sum(g.astype(single), axis=0) for g in grad_branches)

    grad_wout = sum(t_dot(contexts[c], grad_branches[c]) for c in range(clips)).astype(half)
    grad_wout = jnp.concatenate(
        [lax.dynamic_slice_in_dim(grad_wout, (me ^ g) * span, span, 0) for g in range(groups)], axis=0
    )
    quarter = jnp.concatenate([columns(grad_wout, (me ^ r) * span, span) for r in range(groups)], axis=0)
    grad_wout = owned(scatter_sum(quarter))

    grad_qkvs = [
        attend_back(qkvs[c], masks[c], grad_heads[c], sums[c], heads, dim, scale) for c in range(clips)
    ]
    grad_wqkv = owned(sum(t_dot(full1[c], grad_qkvs[c]) for c in range(clips)))
    grad_qkv_bias = sum(jnp.sum(g.astype(single), axis=0) for g in grad_qkvs)
    grad_hidden1 = [scatter_sum(dot_t(grad_qkvs[c], wqkv).astype(half)) for c in range(clips)]
    grad_gain1 = grad_bias1 = 0.0
    grads_in = []
    for c in range(clips):
        gs, gg, gb = norm_back(frames_in[c].astype(single), gain1, bias1, grad_hidden1[c])
        grad_gain1 += gg
        grad_bias1 += gb
        grads_in.append(grad_middles[c] + gs)
    grad_in = jnp.stack(grads_in)

    def rows8(v):
        return v.reshape(owners, depth)

    def spread(v):
        return lax.dynamic_update_slice(jnp.zeros((width,), single), v, (me * span,))

    slot = (jnp.arange(groups) == me).astype(single)[None, :, None]
    rows = jnp.concatenate(
        [rows8(grad_gain1), rows8(grad_bias1), rows8(spread(grad_qkv_bias[:span])),
         rows8(spread(grad_qkv_bias[2 * span :])), rows8(grad_obias), rows8(grad_gain2),
         rows8(grad_bias2), rows8(grad_dbias),
         (grad_ubias.reshape(owners, 1, part) * slot).reshape(owners, units)],
        axis=1,
    )
    rows = jnp.take(rows, own ^ jnp.arange(owners), axis=0)
    bits = owners // 2
    while bits:
        rows = rows[:bits] + flip(rows[bits:], bits, "fsdp")
        bits //= 2
    rows = jnp.concatenate([rows[0], jnp.stack(losses)])
    rows = rows + flip(rows, 1)
    rows = rows + flip(rows, 2)
    small = [rows[k * depth : (k + 1) * depth] for k in range(8)]
    small_up = rows[8 * depth : 8 * depth + units]
    clip_loss = rows[8 * depth + units :]

    def whole(piece):
        return jnp.take(jnp.stack(gather_all(piece)), me ^ jnp.arange(groups), axis=0).astype(single)

    grad_wqkv = whole(grad_wqkv).reshape(groups, depth, 3, span).transpose(1, 2, 0, 3).reshape(depth, 3 * width)
    grad_wout = whole(grad_wout).transpose(1, 0, 2).reshape(depth, width)
    grad_wup = whole(grad_wup).reshape(groups, depth, owners, part).transpose(1, 2, 0, 3).reshape(depth, owners * units)
    grad_wdown = whole(grad_wdown).reshape(units, width)
    return (
        frames_out, clip_loss, grad_in, small[0], small[1], grad_wqkv, small[2], small[3],
        grad_wout, small[4], small[5], small[6], grad_wup, small_up, grad_wdown, small[7],
    )


def solution(mesh):
    vec, mat, act = P("fsdp"), P("fsdp", None), P("fsdp", "seq", None)
    return jax.shard_map(
        local,
        mesh=mesh,
        in_specs=(act, act, P(), vec, vec, mat, vec, vec, mat, vec, vec, vec, mat, vec, mat, vec),
        out_specs=(act, vec, act, vec, vec, mat, vec, vec, mat, vec, vec, vec, mat, vec, mat, vec),
        check_vma=False,
    )
```

```python
import functools
import math

import jax
import jax.numpy as jnp
from jax import lax
from jax.experimental import pallas as pl
from jax.experimental.pallas import tpu as pltpu
from jax.sharding import PartitionSpec as P

HEADS = 16
LANES = 128
LOG2E = 1.0 / math.log(2.0)
single = jnp.float32
half = jnp.bfloat16


def layer_norm(v, gain, bias):
    mean = jnp.mean(v, axis=-1, keepdims=True)
    cent = v - mean
    var = jnp.mean(cent * cent, axis=-1, keepdims=True)
    return cent * lax.rsqrt(var + 1e-05) * gain + bias


def flip(tensor, bits, axis="seq"):
    return lax.ppermute(
        tensor, axis, [(i, i ^ bits) for i in range(lax.axis_size(axis))]
    )


def gather_low(piece, size):
    blocks = {0: piece}
    bits = size // 2
    while bits:
        for r in sorted(blocks):
            blocks[r | bits] = flip(blocks[r], bits)
        bits //= 2
    return [blocks[r] for r in range(size)]


def gather_begin(piece):
    size = lax.axis_size("seq") // 2
    far = flip(piece, size)
    return gather_low(piece, size), far


def gather_end(far):
    return gather_low(far, lax.axis_size("seq") // 2)


def gather_all(piece):
    near, far = gather_begin(piece)
    return near + gather_end(far)


def scatter_terms(make, step):
    groups = lax.axis_size("seq")

    def terms(base, size):
        if size == 1:
            out = make(base)
            step.mark(out)
            return [out]
        near = size // 2
        high = terms(base + near, near)
        if len(high) > 1:
            high = step.after(high[0]).astype(single) + sum(h.astype(single) for h in high[1:])
            high = high.astype(half)
            step.mark(high)
        else:
            high = high[0]
        moved = flip(high, near)
        return terms(base, near) + [moved]

    return terms(0, groups)


def add_terms(parts):
    return sum(p.astype(single) for p in parts)


def swap(parts):
    return [parts[0]] + [flip(parts[r], r) for r in range(1, len(parts))]


def pad_lanes(tensor, tail):
    return jnp.concatenate([tensor, tail], axis=1)


def unit_tail(rows, width):
    lane = lax.broadcasted_iota(jnp.int32, (rows, width), 1)
    return jnp.where(lane == 0, 1.0, 0.0).astype(half)


def attend_kernel(heads, dim, block, scale, qkv_ref, mask_ref, ctx_ref, lse_ref, keys, values):
    seq = qkv_ref.shape[0]
    span = heads * dim
    rest = LANES - dim
    rate = scale * LOG2E
    for j in range(heads):
        keys[j] = pad_lanes(
            qkv_ref[:, span + j * dim : span + (j + 1) * dim], mask_ref[...]
        )
        values[j] = pad_lanes(
            qkv_ref[:, 2 * span + j * dim : 2 * span + (j + 1) * dim], unit_tail(seq, rest)
        )

    def one_block(i, carry):
        rows = pl.ds(pl.multiple_of(i * block, block), block)
        ones = unit_tail(block, rest)
        contexts, sums = [], []
        for j in range(heads):
            query = pad_lanes(qkv_ref[rows, j * dim : (j + 1) * dim], ones)
            scores = lax.dot_general(
                query, keys[j], (((1,), (1,)), ((), ())), preferred_element_type=single
            )
            top = jnp.max(scores, axis=-1, keepdims=True) * rate
            probs = jnp.exp2(scores * rate - top).astype(half)
            mixed = jnp.dot(probs, values[j], preferred_element_type=single)
            total = mixed[:, dim : dim + 1]
            contexts.append((mixed[:, :dim] / total).astype(half))
            sums.append(top + jnp.log(total) * LOG2E)
        ctx_ref[rows, :] = jnp.concatenate(contexts, axis=1)
        lse_ref[rows, :] = jnp.concatenate(sums, axis=1)
        return carry

    lax.fori_loop(0, seq // block, one_block, 0)


def attend_back_kernel(
    heads, dim, block, scale,
    qkv_ref, mask_ref, grad_ref, lse_ref, out_ref, keys, values, gkeys, gvalues, gquery,
):
    seq = qkv_ref.shape[0]
    span = heads * dim
    rest = LANES - dim
    rate = scale * LOG2E
    for j in range(heads):
        keys[j] = pad_lanes(
            qkv_ref[:, span + j * dim : span + (j + 1) * dim], mask_ref[...]
        )
        values[j] = pad_lanes(
            qkv_ref[:, 2 * span + j * dim : 2 * span + (j + 1) * dim],
            jnp.zeros((seq, rest), half),
        )
    gkeys[...] = jnp.zeros_like(gkeys)
    gvalues[...] = jnp.zeros_like(gvalues)

    def one_block(i, carry):
        rows = pl.ds(pl.multiple_of(i * block, block), block)
        ones = unit_tail(block, rest)
        none = jnp.zeros((block, rest), half)
        pieces = []
        for j in range(heads):
            query = pad_lanes(qkv_ref[rows, j * dim : (j + 1) * dim], ones)
            grad = pad_lanes(grad_ref[rows, j * dim : (j + 1) * dim], none)
            scores = lax.dot_general(
                query, keys[j], (((1,), (1,)), ((), ())), preferred_element_type=single
            )
            probs = jnp.exp2(scores * rate - lse_ref[rows, j : j + 1])
            dprobs = lax.dot_general(
                grad, values[j], (((1,), (1,)), ((), ())), preferred_element_type=single
            )
            inner = jnp.sum(probs * dprobs, axis=-1, keepdims=True)
            dscores = (probs * (dprobs - inner)).astype(half)
            pieces.append(
                (jnp.dot(dscores, keys[j], preferred_element_type=single)[:, :dim] * scale).astype(half)
            )
            gkeys[j] += jnp.dot(query.T, dscores, preferred_element_type=single)
            gvalues[j] += jnp.dot(grad.T, probs.astype(half), preferred_element_type=single)
        gquery[rows, :] = jnp.concatenate(pieces, axis=1)
        return carry

    lax.fori_loop(0, seq // block, one_block, 0)

    def put(i, carry):
        rows = pl.ds(pl.multiple_of(i * block, block), block)
        pieces = [gquery[rows, :]]
        for j in range(heads):
            pieces.append((gkeys[j, :, rows].T[:, :dim] * scale).astype(half))
        for j in range(heads):
            pieces.append(gvalues[j, :, rows].T[:, :dim].astype(half))
        out_ref[rows, :] = jnp.concatenate(pieces, axis=1)
        return carry

    lax.fori_loop(0, seq // block, put, 0)


def attend(qkv, mask, heads, dim, scale):
    seq = qkv.shape[0]
    block = 256
    return pl.pallas_call(
        functools.partial(attend_kernel, heads, dim, block, scale),
        out_shape=(
            jax.ShapeDtypeStruct((seq, heads * dim), half),
            jax.ShapeDtypeStruct((seq, heads), single),
        ),
        scratch_shapes=[
            pltpu.VMEM((heads, seq, LANES), half),
            pltpu.VMEM((heads, seq, LANES), half),
        ],
        compiler_params=pltpu.CompilerParams(vmem_limit_bytes=48 << 20),
        cost_estimate=pl.CostEstimate(
            flops=4 * heads * seq * seq * 256, bytes_accessed=qkv.size * 3, transcendentals=heads * seq * seq
        ),
        name="attend",
    )(qkv, mask)


def attend_back(qkv, mask, grad, lse, heads, dim, scale):
    seq = qkv.shape[0]
    block = 256
    return pl.pallas_call(
        functools.partial(attend_back_kernel, heads, dim, block, scale),
        out_shape=jax.ShapeDtypeStruct(qkv.shape, half),
        scratch_shapes=[
            pltpu.VMEM((heads, seq, LANES), half),
            pltpu.VMEM((heads, seq, LANES), half),
            pltpu.VMEM((heads, LANES, seq), single),
            pltpu.VMEM((heads, LANES, seq), single),
            pltpu.VMEM((seq, heads * dim), half),
        ],
        compiler_params=pltpu.CompilerParams(vmem_limit_bytes=56 << 20),
        cost_estimate=pl.CostEstimate(
            flops=10 * heads * seq * seq * 256, bytes_accessed=qkv.size * 5, transcendentals=heads * seq * seq
        ),
        name="attend_back",
    )(qkv, mask, grad, lse)


def norm_kernel(groups, chunk, *refs):
    blocks, gain_ref, bias_ref, out = refs[:groups], refs[groups], refs[groups + 1], refs[groups + 2]
    rows = blocks[0].shape[0]
    for r in range(groups):

        def some(i, carry, r=r):
            start = pl.multiple_of(i * chunk, chunk)
            v = blocks[r][pl.ds(start, chunk), :].astype(single)
            out[pl.ds(r * rows + start, chunk), :] = layer_norm(v, gain_ref[...], bias_ref[...]).astype(half)
            return carry

        lax.fori_loop(0, rows // chunk, some, 0)


def norm_blocks(blocks, gain, bias):
    groups = len(blocks)
    rows, width = blocks[0].shape
    return pl.pallas_call(
        functools.partial(norm_kernel, groups, 64 if rows % 128 else 128),
        out_shape=jax.ShapeDtypeStruct((groups * rows, width), half),
        cost_estimate=pl.CostEstimate(
            flops=groups * rows * width * 10, bytes_accessed=groups * rows * width * 4, transcendentals=0
        ),
        name="norm_blocks",
    )(*blocks, gain, bias)


def products_kernel(pairs, before, beside, *refs):
    lefts, rights = refs[:pairs], refs[pairs : 2 * pairs]
    more, out = refs[2 * pairs : -1], refs[-1]
    total = more[0][...] if before else None
    for a, b in zip(lefts, rights):
        term = lax.dot_general(
            a[...], b[...], (((0,), (0,)), ((), ())), preferred_element_type=single
        )
        total = term if total is None else total + term
    total = total.astype(out.dtype)
    if beside:
        total = jnp.concatenate([total, more[-1][...]], axis=1)
    out[...] = total


def products(lefts, rights, kind, before=None, beside=None, into=None, slot=0, slots=1):
    pairs = len(lefts)
    rows, cols = lefts[0].shape[1], rights[0].shape[1]
    tile = next(t for t in (256, 128, rows) if rows % t == 0)
    depth = sum(a.shape[0] for a in lefts)
    in_specs = [pl.BlockSpec((a.shape[0], tile), lambda i: (0, i)) for a in lefts]
    in_specs += [pl.BlockSpec(b.shape, lambda i: (0, 0)) for b in rights]
    more = []
    if before is not None:
        more.append(before)
        in_specs.append(pl.BlockSpec((tile, cols), lambda i: (i, 0)))
    if beside is not None:
        more.append(beside)
        in_specs.append(pl.BlockSpec((tile, beside.shape[1]), lambda i: (i, 0)))
        cols += beside.shape[1]
    body = functools.partial(products_kernel, pairs, before is not None, beside is not None)
    aliases = {}
    if into is not None:
        aliases = {2 * pairs + len(more): 0}
        more.append(into)
        in_specs.append(pl.BlockSpec(memory_space=pl.ANY))
        inner = body

        def body(*refs):
            inner(*refs[:-2], refs[-1])

    return pl.pallas_call(
        body,
        grid=(rows // tile,),
        in_specs=in_specs,
        out_specs=pl.BlockSpec((tile, cols), lambda i: (i, slot)),
        out_shape=jax.ShapeDtypeStruct((rows, cols * slots), kind),
        input_output_aliases=aliases,
        compiler_params=pltpu.CompilerParams(vmem_limit_bytes=56 << 20),
        cost_estimate=pl.CostEstimate(
            flops=2 * depth * rows * cols, bytes_accessed=2 * depth * (rows + cols), transcendentals=0
        ),
        name="products",
    )(*lefts, *rights, *more)


def assemble_kernel(groups, counts, width, me_ref, *refs):
    pieces, out = refs[:groups], refs[groups]
    rows = pieces[0].shape[0]
    for v in range(groups):

        @pl.when(me_ref[0] == v)
        def _():
            for g in range(groups):
                piece = pieces[v ^ g]
                if counts == 0:
                    out[g * rows : (g + 1) * rows, :] = piece[...].astype(single)
            if counts:
                blocks = [
                    pieces[v ^ g][:, k * width : (k + 1) * width]
                    for k in range(counts)
                    for g in range(groups)
                ]
                out[...] = jnp.concatenate(blocks, axis=1).astype(single)


def assemble(pieces, counts, me):
    groups = len(pieces)
    rows, cols = pieces[0].shape
    shape = (rows, cols * groups) if counts else (rows * groups, cols)
    return pl.pallas_call(
        functools.partial(assemble_kernel, groups, counts, cols // max(counts, 1)),
        out_shape=jax.ShapeDtypeStruct(shape, single),
        in_specs=[pl.BlockSpec(memory_space=pltpu.SMEM)]
        + [pl.BlockSpec(memory_space=pltpu.VMEM)] * groups,
        cost_estimate=pl.CostEstimate(
            flops=0, bytes_accessed=rows * cols * groups * 6, transcendentals=0
        ),
        name="assemble",
    )(me.astype(jnp.int32).reshape(1), *pieces)


def gather_blocks_kernel(groups, me_ref, *refs):
    pieces, out = refs[:groups], refs[groups]
    span = pieces[0].shape[1]
    for v in range(groups):

        @pl.when(me_ref[0] == v)
        def _():
            for r in range(groups):
                rows = [
                    pieces[v ^ g][(v ^ r) * span : ((v ^ r) + 1) * span, :] for g in range(groups)
                ]
                out[r * span : (r + 1) * span, :] = jnp.concatenate(rows, axis=1)


def scatter_blocks_kernel(groups, me_ref, full, *outs):
    span = outs[0].shape[1]
    for v in range(groups):

        @pl.when(me_ref[0] == v)
        def _():
            for r in range(groups):
                for g in range(groups):
                    outs[r][g * span : (g + 1) * span, :] = full[
                        (v ^ g) * span : ((v ^ g) + 1) * span, (v ^ r) * span : ((v ^ r) + 1) * span
                    ]


def arrange(kernel, arrays, shapes, groups, me, name):
    return pl.pallas_call(
        functools.partial(kernel, groups),
        out_shape=shapes,
        in_specs=[pl.BlockSpec(memory_space=pltpu.SMEM)]
        + [pl.BlockSpec(memory_space=pltpu.VMEM)] * len(arrays),
        cost_estimate=pl.CostEstimate(
            flops=0, bytes_accessed=sum(x.size for x in arrays) * 4, transcendentals=0
        ),
        name=name,
    )(me.astype(jnp.int32).reshape(1), *arrays)


class Order:
    def __init__(self):
        self.tokens = []

    def after(self, tensor):
        if not self.tokens:
            return tensor
        return lax.optimization_barrier((tensor, *self.tokens))[0]

    def mark(self, *tensors):
        self.tokens = list(tensors)

    def also(self, *tensors):
        self.tokens += tensors


def local(
    frames_in, teacher, lengths, norm1_gain, norm1_bias, w_qkv, query_bias, value_bias,
    w_attn_out, attn_out_bias, norm2_gain, norm2_bias, w_up, up_bias, w_down, down_bias,
):
    clips, frames, width = frames_in.shape
    groups = lax.axis_size("seq")
    owners = lax.axis_size("fsdp")
    me = lax.axis_index("seq")
    own = lax.axis_index("fsdp")
    seq_len = frames * groups
    dim = width // HEADS
    heads = HEADS // groups
    span = heads * dim
    depth = w_qkv.shape[0]
    units = w_down.shape[0]
    part = units // groups
    scale = 1.0 / math.sqrt(dim)

    def dot(a, b):
        return jnp.dot(a, b, preferred_element_type=single)

    def dot_t(a, b):
        return lax.dot_general(a, b, (((1,), (1,)), ((), ())), preferred_element_type=single)

    def t_dot(a, b):
        return lax.dot_general(a, b, (((0,), (0,)), ((), ())), preferred_element_type=single)

    def columns(array, start, size):
        return lax.dynamic_slice_in_dim(array, start, size, 1)

    def butterfly(array):
        bits = 1
        while bits < owners:
            array = jnp.concatenate([array, flip(array, bits, "fsdp")], axis=0)
            bits *= 2
        return [
            lax.dynamic_index_in_dim(array, own ^ f, 0, keepdims=False) for f in range(owners)
        ]

    ff = owners * part
    first = jnp.concatenate(
        [columns(w_qkv, k * width + me * span, span) for k in range(3)]
        + [columns(w_attn_out, me * span, span)],
        axis=1,
    )
    first = lax.all_gather(first, "fsdp", axis=0, tiled=True)
    wqkv = first[:, : 3 * span]
    wup = jnp.concatenate([columns(w_up, f * units + me * part, part) for f in range(owners)], axis=1)
    wdown = lax.dynamic_slice_in_dim(w_down, me * part, part, 0)
    if part == depth:
        second = lax.all_gather(jnp.concatenate([wup, wdown], axis=1), "fsdp", axis=0, tiled=True)
        wup, wdown = second[:, :ff], second[:, ff:]
    else:
        wup = lax.all_gather(wup, "fsdp", axis=0, tiled=True)
        wdown = lax.all_gather(wdown, "fsdp", axis=0, tiled=True)

    states = []
    for c in range(clips):
        piece = frames_in[c]
        if states:
            piece = lax.optimization_barrier((piece, states[-1][0][-1]))[0]
        states.append(gather_begin(piece))

    packed = jnp.concatenate(
        [norm1_gain, norm1_bias, query_bias, value_bias, attn_out_bias, norm2_gain, norm2_bias,
         down_bias, up_bias]
    )[None]
    vectors = jnp.stack(butterfly(packed)).astype(single)

    def vector(k):
        return vectors[:, k * depth : (k + 1) * depth].reshape(1, width)

    gain1, bias1, qbias, vbias, obias, gain2, bias2, dbias = (vector(k) for k in range(8))
    ubias = lax.dynamic_slice_in_dim(vectors, 8 * depth + me * part, part, 1).reshape(1, ff)
    qkv_bias = jnp.concatenate(
        [columns(qbias, me * span, span), jnp.zeros((1, span), single), columns(vbias, me * span, span)],
        axis=1,
    )

    quarters = gather_all(first[:, 3 * span :])

    mine = lax.dynamic_slice_in_dim(lengths, own * clips, clips)
    order = (me ^ jnp.arange(groups, dtype=jnp.int32))[:, None] * frames + jnp.arange(
        frames, dtype=jnp.int32
    )
    order = order.reshape(seq_len)
    count = jnp.sum(lengths).astype(single)
    lane0 = (jnp.arange(LANES - dim) == 0)[None, :]
    masks = [
        jnp.where((order >= mine[c])[:, None] & lane0, -1e30, 0.0).astype(half) for c in range(clips)
    ]
    row_valid = [(order[:frames] < mine[c]).astype(single)[:, None] for c in range(clips)]

    step = Order()

    n = frames
    every = range(clips)
    full1 = [None] * clips
    qkvs, sums, moved, contexts = ([None] * clips for _ in range(4))
    middles, hiddens, actives, slopes, branches = ([None] * clips for _ in range(5))
    outs, losses, grad_outs, pieces = ([None] * clips for _ in range(4))
    grad_uppers, grad_hidden2, grad_middles, grad_branches = ([None] * clips for _ in range(4))
    grad_heads, grad_qkvs, grad_hidden1, grads_in = ([None] * clips for _ in range(4))
    norm2_grads, norm1_grads = [None] * clips, [None] * clips

    def rows_of(array, r):
        return array[r * n : (r + 1) * n]

    def owned(grad):
        return lax.psum_scatter(grad, "fsdp", scatter_dimension=0, tiled=True)

    def norm_back(v, gain, bias, grad):
        _, back = jax.vjp(layer_norm, v, gain, bias)
        return back(grad)

    def arriving(store, c):
        near, far = store[c]
        yield from near
        far = gather_end(step.after(far))
        store[c] = near + far
        yield from far

    def norm1(c):
        near, far = states[c]
        full1[c] = norm_blocks(near + gather_end(step.after(far)), gain1, bias1)
        step.mark(full1[c])

    def attention(c):
        qkvs[c] = (dot(step.after(full1[c]), wqkv) + qkv_bias).astype(half)
        context, sums[c] = attend(qkvs[c], masks[c], heads, dim, scale)
        parts = [rows_of(context, r) for r in range(groups)]
        step.mark(*parts)
        moved[c] = swap(parts)

    def project(c):
        contexts[c] = jnp.concatenate([step.after(moved[c][0])] + moved[c][1:], axis=1)
        middles[c] = frames_in[c].astype(single) + dot(contexts[c], wout) + obias
        hidden = layer_norm(middles[c], gain2, bias2).astype(half)
        step.mark(hidden)
        hiddens[c] = gather_begin(hidden)

    def up(c):
        actives[c], slopes[c] = [], []
        for block in arriving(hiddens, c):
            upper = dot(step.after(block), wup) + ubias
            cdf = 0.5 * (1.0 + lax.erf(upper * math.sqrt(0.5)))
            actives[c].append((upper * cdf).astype(half))
            slopes[c].append(
                (cdf + upper * (jnp.exp(-0.5 * upper * upper) * (1.0 / math.sqrt(2.0 * math.pi)))).astype(half)
            )
            step.mark(actives[c][-1])

    def down(c):
        branches[c] = scatter_terms(
            lambda r: dot(step.after(actives[c][r]), wdown).astype(half), step
        )

    def loss(c):
        result = step.after(middles[c]) + add_terms(branches[c]) + dbias
        outs[c] = result.astype(half)
        diff = result - teacher[c].astype(single)
        masked = diff * row_valid[c]
        losses[c] = jnp.sum(masked * diff) / (2.0 * width * count)
        grad_outs[c] = masked * (float(lengths.shape[0] * seq_len) / count)
        branch = grad_outs[c].astype(half)
        step.mark(branch)
        pieces[c] = gather_begin(branch)

    def back_up(c):
        grad_uppers[c] = []
        for block in arriving(pieces, c):
            grad = dot_t(step.after(block), wdown) * slopes[c][len(grad_uppers[c])].astype(single)
            grad_uppers[c].append(grad.astype(half))
            step.mark(grad_uppers[c][-1])

    def back_down(c):
        grad_hidden2[c] = scatter_terms(
            lambda r: dot_t(step.after(grad_uppers[c][r]), wup).astype(half), step
        )

    def norm2(c):
        gm, *norm2_grads[c] = norm_back(
            step.after(middles[c]), gain2, bias2, add_terms(grad_hidden2[c])
        )
        grad_middles[c] = grad_outs[c] + gm
        grad_branches[c] = grad_middles[c].astype(half)
        grad_context = dot_t(grad_branches[c], wout).astype(half)
        parts = [grad_context[:, r * span : (r + 1) * span] for r in range(groups)]
        step.mark(*parts)
        grad_heads[c] = swap(parts)

    def attention_back(c):
        grad_head = jnp.concatenate([step.after(grad_heads[c][0])] + grad_heads[c][1:], axis=0)
        grad_qkvs[c] = attend_back(qkvs[c], masks[c], grad_head, sums[c], heads, dim, scale)
        step.mark(grad_qkvs[c])

    def hidden_back(c):
        grad_hidden1[c] = scatter_terms(
            lambda r: dot_t(rows_of(step.after(grad_qkvs[c]), r), wqkv).astype(half), step
        )

    def norm1_back(c):
        gs, *norm1_grads[c] = norm_back(
            step.after(frames_in[c]).astype(single), gain1, bias1, add_terms(grad_hidden1[c])
        )
        grads_in[c] = grad_middles[c] + gs
        step.mark(grads_in[c])

    first_clip, *others = every
    for c in every:
        norm1(c)
    attention(first_clip)
    wout = arrange(
        gather_blocks_kernel, quarters, jax.ShapeDtypeStruct((width, width), half), groups, me,
        "place_output_weight",
    )
    for c in others:
        attention(c)
    for c in every:
        project(c)
    for c in every:
        up(c)
        down(c)
    for c in every:
        loss(c)
    for c in every:
        back_up(c)
        back_down(c)

    def flat(store):
        return [x for blocks in store for x in blocks]

    def ordered(lefts):
        return [step.after(lefts[0])] + lefts[1:]

    joined = part == depth
    grad_wdown = products(ordered(flat(actives)), flat(pieces), half, slots=1 + joined)
    step.mark(grad_wdown)
    norm2(first_clip)
    grad_wup = products(
        ordered(flat(hiddens)), flat(grad_uppers), half,
        **(dict(into=grad_wdown, slot=1, slots=2) if joined else {}),
    )
    step.mark(grad_wup)
    if joined:
        both = owned(grad_wup)
        grad_wdown, grad_wup = both[:, :width], both[:, width:]
    else:
        grad_wdown, grad_wup = owned(grad_wdown), owned(grad_wup)
    for c in others:
        norm2(c)
    grad_wout = products(ordered(contexts), grad_branches, half)
    step.mark(grad_wout)
    quarters = arrange(
        scatter_blocks_kernel, [grad_wout],
        [jax.ShapeDtypeStruct((width, span), half)] * groups, groups, me, "split_output_weight",
    )
    attention_back(first_clip)
    hidden_back(first_clip)
    early = products(ordered(full1[:-1]), grad_qkvs[:-1], single)
    step.mark(early)
    grad_wout = scatter_terms(lambda r: quarters[r], Order())
    grad_wout = add_terms([step.after(grad_wout[0])] + grad_wout[1:]).astype(half)
    step.mark(grad_wout)
    for c in others:
        attention_back(c)
    step.also(grad_wup)
    total = products(ordered(full1[-1:]), grad_qkvs[-1:], half, before=early, beside=grad_wout)
    step.mark(total)
    total = owned(total)
    grad_wqkv, grad_wout = total[:, : 3 * span], total[:, 3 * span :]
    for c in others:
        hidden_back(c)
    for c in every:
        norm1_back(c)
    frames_out = jnp.stack(outs)
    grad_in = jnp.stack(grads_in)
    grad_gain1, grad_bias1 = (sum(g) for g in zip(*norm1_grads))
    grad_gain2, grad_bias2 = (sum(g) for g in zip(*norm2_grads))
    grad_dbias = sum(jnp.sum(g.astype(half).astype(single), axis=0) for g in grad_outs)
    grad_ubias = sum(jnp.sum(g.astype(single), axis=0) for blocks in grad_uppers for g in blocks)
    grad_obias = sum(jnp.sum(g.astype(single), axis=0) for g in grad_branches)
    grad_qkv_bias = sum(jnp.sum(g.astype(single), axis=0) for g in grad_qkvs)

    def rows8(v):
        return v.reshape(owners, depth)

    def spread(v):
        return lax.dynamic_update_slice(jnp.zeros((width,), single), v, (me * span,))

    slot = (jnp.arange(groups) == me).astype(single)[None, :, None]
    rows = jnp.concatenate(
        [rows8(grad_gain1), rows8(grad_bias1), rows8(spread(grad_qkv_bias[:span])),
         rows8(spread(grad_qkv_bias[2 * span :])), rows8(grad_obias), rows8(grad_gain2),
         rows8(grad_bias2), rows8(grad_dbias),
         (grad_ubias.reshape(owners, 1, part) * slot).reshape(owners, units)],
        axis=1,
    )
    rows = jnp.take(rows, own ^ jnp.arange(owners), axis=0)
    bits = owners // 2
    while bits:
        rows = rows[:bits] + flip(rows[bits:], bits, "fsdp")
        bits //= 2
    rows = jnp.concatenate([rows[0], jnp.stack(losses)])
    rows = rows + flip(rows, 1)
    rows = rows + flip(rows, 2)
    small = [rows[k * depth : (k + 1) * depth] for k in range(8)]
    small_up = rows[8 * depth : 8 * depth + units]
    clip_loss = rows[8 * depth + units :]

    grad_wdown = assemble(gather_all(grad_wdown), 0, me)
    grad_wup = assemble(gather_all(grad_wup), owners, me)
    grad_wqkv = assemble(gather_all(grad_wqkv), 3, me)
    grad_wout = assemble(gather_all(grad_wout), 1, me)
    return (
        frames_out, clip_loss, grad_in, small[0], small[1], grad_wqkv, small[2], small[3],
        grad_wout, small[4], small[5], small[6], grad_wup, small_up, grad_wdown, small[7],
    )


def solution(mesh):
    vec, mat, act = P("fsdp"), P("fsdp", None), P("fsdp", "seq", None)
    return jax.shard_map(
        local,
        mesh=mesh,
        in_specs=(act, act, P(), vec, vec, mat, vec, vec, mat, vec, vec, vec, mat, vec, mat, vec),
        out_specs=(act, vec, act, vec, vec, mat, vec, vec, mat, vec, vec, vec, mat, vec, mat, vec),
        check_vma=False,
    )
```

```python
import functools
import math

import jax
import jax.numpy as jnp
from jax import lax
from jax.experimental import pallas as pl
from jax.experimental.pallas import tpu as pltpu
from jax.sharding import PartitionSpec as P

HEADS = 16
LANES = 128
LOG2E = 1.0 / math.log(2.0)
single = jnp.float32
half = jnp.bfloat16


def norm_stats(v):
    mean = jnp.mean(v, axis=-1, keepdims=True)
    cent = v - mean
    var = jnp.mean(cent * cent, axis=-1, keepdims=True)
    return mean, lax.rsqrt(var + 1e-05)


def layer_norm(v, stats, gain, bias):
    return (v - stats[0]) * stats[1] * gain + bias


def norm_back(v, stats, gain, grad):
    scaled = (v - stats[0]) * stats[1]
    inner = grad * gain
    first = jnp.mean(inner, axis=-1, keepdims=True)
    second = jnp.mean(inner * scaled, axis=-1, keepdims=True)
    return (
        stats[1] * (inner - first - scaled * second),
        jnp.sum(grad * scaled, axis=0),
        jnp.sum(grad, axis=0),
    )


def flip(tensor, bits, axis="seq"):
    return lax.ppermute(
        tensor, axis, [(i, i ^ bits) for i in range(lax.axis_size(axis))]
    )


def gather_low(piece, size):
    blocks = {0: piece}
    bits = size // 2
    while bits:
        for r in sorted(blocks):
            blocks[r | bits] = flip(blocks[r], bits)
        bits //= 2
    return [blocks[r] for r in range(size)]


def gather_begin(piece):
    size = lax.axis_size("seq") // 2
    far = flip(piece, size)
    return gather_low(piece, size), far


def gather_end(far):
    return gather_low(far, lax.axis_size("seq") // 2)


def gather_all(piece):
    near, far = gather_begin(piece)
    return near + gather_end(far)


def scatter_terms(make, step):
    groups = lax.axis_size("seq")

    def terms(base, size):
        if size == 1:
            out = make(base)
            step.mark(out)
            return [out]
        near = size // 2
        high = terms(base + near, near)
        if len(high) > 1:
            high = step.after(high[0]).astype(single) + sum(h.astype(single) for h in high[1:])
            high = high.astype(half)
            step.mark(high)
        else:
            high = high[0]
        moved = flip(high, near)
        return terms(base, near) + [moved]

    return terms(0, groups)


def add_terms(parts):
    return sum(p.astype(single) for p in parts)


def swap(parts):
    return [parts[0]] + [flip(parts[r], r) for r in range(1, len(parts))]


def pad_lanes(tensor, tail):
    return jnp.concatenate([tensor, tail], axis=1)


def unit_tail(rows, width):
    lane = lax.broadcasted_iota(jnp.int32, (rows, width), 1)
    return jnp.where(lane == 0, 1.0, 0.0).astype(half)


def attend_kernel(heads, dim, block, scale, qkv_ref, mask_ref, ctx_ref, lse_ref, keys, values):
    seq = qkv_ref.shape[0]
    span = heads * dim
    rest = LANES - dim
    rate = scale * LOG2E
    for j in range(heads):
        keys[j] = pad_lanes(
            qkv_ref[:, span + j * dim : span + (j + 1) * dim], mask_ref[...]
        )
        values[j] = pad_lanes(
            qkv_ref[:, 2 * span + j * dim : 2 * span + (j + 1) * dim], unit_tail(seq, rest)
        )

    def one_block(i, carry):
        rows = pl.ds(pl.multiple_of(i * block, block), block)
        ones = unit_tail(block, rest)
        contexts, sums = [], []
        for j in range(heads):
            query = pad_lanes(qkv_ref[rows, j * dim : (j + 1) * dim], ones)
            scores = lax.dot_general(
                query, keys[j], (((1,), (1,)), ((), ())), preferred_element_type=single
            )
            top = jnp.max(scores, axis=-1, keepdims=True) * rate
            probs = jnp.exp2(scores * rate - top).astype(half)
            mixed = jnp.dot(probs, values[j], preferred_element_type=single)
            total = mixed[:, dim : dim + 1]
            contexts.append((mixed[:, :dim] / total).astype(half))
            sums.append(top + jnp.log(total) * LOG2E)
        ctx_ref[rows, :] = jnp.concatenate(contexts, axis=1)
        lse_ref[rows, :] = jnp.concatenate(sums, axis=1)
        return carry

    lax.fori_loop(0, seq // block, one_block, 0)


def attend_back_kernel(
    heads, dim, block, scale,
    qkv_ref, mask_ref, grad_ref, lse_ref, out_ref, keys, values, gkeys, gvalues, gquery,
):
    seq = qkv_ref.shape[0]
    span = heads * dim
    rest = LANES - dim
    rate = scale * LOG2E
    for j in range(heads):
        keys[j] = pad_lanes(
            qkv_ref[:, span + j * dim : span + (j + 1) * dim], mask_ref[...]
        )
        values[j] = pad_lanes(
            qkv_ref[:, 2 * span + j * dim : 2 * span + (j + 1) * dim],
            jnp.zeros((seq, rest), half),
        )
    gkeys[...] = jnp.zeros_like(gkeys)
    gvalues[...] = jnp.zeros_like(gvalues)

    def one_block(i, carry):
        rows = pl.ds(pl.multiple_of(i * block, block), block)
        ones = unit_tail(block, rest)
        none = jnp.zeros((block, rest), half)
        pieces = []
        for j in range(heads):
            query = pad_lanes(qkv_ref[rows, j * dim : (j + 1) * dim], ones)
            grad = pad_lanes(grad_ref[rows, j * dim : (j + 1) * dim], none)
            scores = lax.dot_general(
                query, keys[j], (((1,), (1,)), ((), ())), preferred_element_type=single
            )
            probs = jnp.exp2(scores * rate - lse_ref[rows, j : j + 1])
            dprobs = lax.dot_general(
                grad, values[j], (((1,), (1,)), ((), ())), preferred_element_type=single
            )
            inner = jnp.sum(probs * dprobs, axis=-1, keepdims=True)
            dscores = (probs * (dprobs - inner)).astype(half)
            pieces.append(
                (jnp.dot(dscores, keys[j], preferred_element_type=single)[:, :dim] * scale).astype(half)
            )
            gkeys[j] += jnp.dot(query.T, dscores, preferred_element_type=single)
            gvalues[j] += jnp.dot(grad.T, probs.astype(half), preferred_element_type=single)
        gquery[rows, :] = jnp.concatenate(pieces, axis=1)
        return carry

    lax.fori_loop(0, seq // block, one_block, 0)

    def put(i, carry):
        rows = pl.ds(pl.multiple_of(i * block, block), block)
        pieces = [gquery[rows, :]]
        for j in range(heads):
            pieces.append((gkeys[j, :, rows].T[:, :dim] * scale).astype(half))
        for j in range(heads):
            pieces.append(gvalues[j, :, rows].T[:, :dim].astype(half))
        out_ref[rows, :] = jnp.concatenate(pieces, axis=1)
        return carry

    lax.fori_loop(0, seq // block, put, 0)


def attend(qkv, mask, heads, dim, scale):
    seq = qkv.shape[0]
    block = 256
    return pl.pallas_call(
        functools.partial(attend_kernel, heads, dim, block, scale),
        out_shape=(
            jax.ShapeDtypeStruct((seq, heads * dim), half),
            jax.ShapeDtypeStruct((seq, heads), single),
        ),
        scratch_shapes=[
            pltpu.VMEM((heads, seq, LANES), half),
            pltpu.VMEM((heads, seq, LANES), half),
        ],
        compiler_params=pltpu.CompilerParams(vmem_limit_bytes=48 << 20),
        cost_estimate=pl.CostEstimate(
            flops=4 * heads * seq * seq * 256, bytes_accessed=qkv.size * 3, transcendentals=heads * seq * seq
        ),
        name="attend",
    )(qkv, mask)


def attend_back(qkv, mask, grad, lse, heads, dim, scale):
    seq = qkv.shape[0]
    block = 256
    return pl.pallas_call(
        functools.partial(attend_back_kernel, heads, dim, block, scale),
        out_shape=jax.ShapeDtypeStruct(qkv.shape, half),
        scratch_shapes=[
            pltpu.VMEM((heads, seq, LANES), half),
            pltpu.VMEM((heads, seq, LANES), half),
            pltpu.VMEM((heads, LANES, seq), single),
            pltpu.VMEM((heads, LANES, seq), single),
            pltpu.VMEM((seq, heads * dim), half),
        ],
        compiler_params=pltpu.CompilerParams(vmem_limit_bytes=56 << 20),
        cost_estimate=pl.CostEstimate(
            flops=20 * heads * seq * seq * 256, bytes_accessed=qkv.size * 5, transcendentals=heads * seq * seq
        ),
        name="attend_back",
    )(qkv, mask, grad, lse)


def norm_kernel(groups, chunk, *refs):
    blocks, gain_ref, bias_ref, out = refs[:groups], refs[groups], refs[groups + 1], refs[groups + 2]
    rows = blocks[0].shape[0]
    for r in range(groups):

        def some(i, carry, r=r):
            start = pl.multiple_of(i * chunk, chunk)
            v = blocks[r][pl.ds(start, chunk), :].astype(single)
            out[pl.ds(r * rows + start, chunk), :] = layer_norm(v, norm_stats(v), gain_ref[...], bias_ref[...]).astype(
                half
            )
            return carry

        lax.fori_loop(0, rows // chunk, some, 0)


def norm_blocks(blocks, gain, bias):
    groups = len(blocks)
    rows, width = blocks[0].shape
    return pl.pallas_call(
        functools.partial(norm_kernel, groups, 64 if rows % 128 else 128),
        out_shape=jax.ShapeDtypeStruct((groups * rows, width), half),
        cost_estimate=pl.CostEstimate(
            flops=groups * rows * width * 10, bytes_accessed=groups * rows * width * 4, transcendentals=0
        ),
        name="norm_blocks",
    )(*blocks, gain, bias)


def products_kernel(pairs, before, beside, *refs):
    lefts, rights = refs[:pairs], refs[pairs : 2 * pairs]
    more, out = refs[2 * pairs : -1], refs[-1]
    total = more[0][...] if before else None
    for a, b in zip(lefts, rights):
        term = lax.dot_general(
            a[...], b[...], (((0,), (0,)), ((), ())), preferred_element_type=single
        )
        total = term if total is None else total + term
    total = total.astype(out.dtype)
    if beside:
        total = jnp.concatenate([total, more[-1][:, :beside]], axis=1)
    out[...] = total


def products(lefts, rights, kind, before=None, beside=None, width=0, into=None, slot=0, slots=1):
    pairs = len(lefts)
    rows, cols = lefts[0].shape[1], rights[0].shape[1]
    tile = next(t for t in (256, 128, rows) if rows % t == 0)
    depth = sum(a.shape[0] for a in lefts)
    in_specs = [pl.BlockSpec((a.shape[0], tile), lambda i: (0, i)) for a in lefts]
    in_specs += [pl.BlockSpec(b.shape, lambda i: (0, 0)) for b in rights]
    more = []
    if before is not None:
        more.append(before)
        in_specs.append(pl.BlockSpec((tile, cols), lambda i: (i, 0)))
    if beside is not None:
        more.append(beside)
        in_specs.append(pl.BlockSpec((tile, beside.shape[1]), lambda i: (i, 0)))
        cols += width
    body = functools.partial(products_kernel, pairs, before is not None, width)
    aliases = {}
    if into is not None:
        aliases = {2 * pairs + len(more): 0}
        more.append(into)
        in_specs.append(pl.BlockSpec(memory_space=pl.ANY))
        inner = body

        def body(*refs):
            inner(*refs[:-2], refs[-1])

    return pl.pallas_call(
        body,
        grid=(rows // tile,),
        in_specs=in_specs,
        out_specs=pl.BlockSpec((tile, cols), lambda i: (i, slot)),
        out_shape=jax.ShapeDtypeStruct((rows, cols * slots), kind),
        input_output_aliases=aliases,
        compiler_params=pltpu.CompilerParams(vmem_limit_bytes=56 << 20),
        cost_estimate=pl.CostEstimate(
            flops=2 * depth * rows * cols, bytes_accessed=2 * depth * (rows + cols), transcendentals=0
        ),
        name="products",
    )(*lefts, *rights, *more)


def spread_kernel(grad, weight, *outs):
    n = outs[0].shape[0]
    for r, out in enumerate(outs):
        out[...] = lax.dot_general(
            grad[r * n : (r + 1) * n, :], weight[...], (((1,), (1,)), ((), ())),
            preferred_element_type=single,
        ).astype(half)


def spread_terms(grad, weight, groups):
    rows, cols = grad.shape[0] // groups, weight.shape[0]
    return pl.pallas_call(
        spread_kernel,
        out_shape=[jax.ShapeDtypeStruct((rows, cols), half)] * groups,
        compiler_params=pltpu.CompilerParams(vmem_limit_bytes=32 << 20),
        cost_estimate=pl.CostEstimate(flops=0, bytes_accessed=0, transcendentals=0),
        name="spread_terms",
    )(grad, weight)


def assemble_kernel(groups, counts, width, start, me_ref, *refs):
    pieces, out = refs[:groups], refs[groups]
    rows = pieces[0].shape[0]
    for v in range(groups):

        @pl.when(me_ref[0] == v)
        def _():
            for g in range(groups):
                piece = pieces[v ^ g]
                if counts == 0:
                    out[g * rows : (g + 1) * rows, :] = piece[...].astype(single)
            if counts:
                blocks = [
                    pieces[v ^ g][:, start + k * width : start + (k + 1) * width]
                    for k in range(counts)
                    for g in range(groups)
                ]
                out[...] = jnp.concatenate(blocks, axis=1).astype(single)


def assemble(pieces, counts, me, start=0, cols=None):
    groups = len(pieces)
    rows = pieces[0].shape[0]
    cols = cols or pieces[0].shape[1]
    shape = (rows, cols * groups) if counts else (rows * groups, cols)
    return pl.pallas_call(
        functools.partial(assemble_kernel, groups, counts, cols // max(counts, 1), start),
        out_shape=jax.ShapeDtypeStruct(shape, single),
        in_specs=[pl.BlockSpec(memory_space=pltpu.SMEM)]
        + [pl.BlockSpec(memory_space=pltpu.VMEM)] * groups,
        cost_estimate=pl.CostEstimate(
            flops=0, bytes_accessed=rows * cols * groups * 6, transcendentals=0
        ),
        name="assemble",
    )(me.astype(jnp.int32).reshape(1), *pieces)


def gather_blocks_kernel(groups, me_ref, *refs):
    pieces, out = refs[:groups], refs[groups]
    span = pieces[0].shape[1]
    for v in range(groups):

        @pl.when(me_ref[0] == v)
        def _():
            for r in range(groups):
                rows = [
                    pieces[v ^ g][(v ^ r) * span : ((v ^ r) + 1) * span, :] for g in range(groups)
                ]
                out[r * span : (r + 1) * span, :] = jnp.concatenate(rows, axis=1)


def scatter_blocks_kernel(groups, me_ref, full, *outs):
    span = full.shape[1] // groups
    spare = outs[0].shape[1] - span
    for v in range(groups):

        @pl.when(me_ref[0] == v)
        def _():
            for r in range(groups):
                for g in range(groups):
                    block = full[
                        (v ^ g) * span : ((v ^ g) + 1) * span, (v ^ r) * span : ((v ^ r) + 1) * span
                    ]
                    if spare:
                        block = jnp.concatenate([block, jnp.zeros((span, spare), block.dtype)], axis=1)
                    outs[r][g * span : (g + 1) * span, :] = block


def arrange(kernel, arrays, shapes, groups, me, name):
    return pl.pallas_call(
        functools.partial(kernel, groups),
        out_shape=shapes,
        in_specs=[pl.BlockSpec(memory_space=pltpu.SMEM)]
        + [pl.BlockSpec(memory_space=pltpu.VMEM)] * len(arrays),
        cost_estimate=pl.CostEstimate(
            flops=0, bytes_accessed=sum(x.size for x in arrays) * 4, transcendentals=0
        ),
        name=name,
    )(me.astype(jnp.int32).reshape(1), *arrays)


class Order:
    def __init__(self):
        self.tokens = []

    def after(self, tensor):
        if not self.tokens:
            return tensor
        return lax.optimization_barrier((tensor, *self.tokens))[0]

    def after_all(self, tensors):
        return list(lax.optimization_barrier((*tensors, *self.tokens))[: len(tensors)])

    def mark(self, *tensors):
        self.tokens = list(tensors)

    def also(self, *tensors):
        self.tokens += tensors


def local(
    frames_in, teacher, lengths, norm1_gain, norm1_bias, w_qkv, query_bias, value_bias,
    w_attn_out, attn_out_bias, norm2_gain, norm2_bias, w_up, up_bias, w_down, down_bias,
):
    clips, frames, width = frames_in.shape
    groups = lax.axis_size("seq")
    owners = lax.axis_size("fsdp")
    me = lax.axis_index("seq")
    own = lax.axis_index("fsdp")
    seq_len = frames * groups
    dim = width // HEADS
    heads = HEADS // groups
    span = heads * dim
    depth = w_qkv.shape[0]
    units = w_down.shape[0]
    part = units // groups
    scale = 1.0 / math.sqrt(dim)

    def dot(a, b):
        return jnp.dot(a, b, preferred_element_type=single)

    def dot_t(a, b):
        return lax.dot_general(a, b, (((1,), (1,)), ((), ())), preferred_element_type=single)

    def t_dot(a, b):
        return lax.dot_general(a, b, (((0,), (0,)), ((), ())), preferred_element_type=single)

    def columns(array, start, size):
        return lax.dynamic_slice_in_dim(array, start, size, 1)

    def butterfly(array):
        bits = 1
        while bits < owners:
            array = jnp.concatenate([array, flip(array, bits, "fsdp")], axis=0)
            bits *= 2
        return [
            lax.dynamic_index_in_dim(array, own ^ f, 0, keepdims=False) for f in range(owners)
        ]

    ff = owners * part
    first = jnp.concatenate(
        [columns(w_qkv, k * width + me * span, span) for k in range(3)]
        + [columns(w_attn_out, me * span, span)],
        axis=1,
    )
    first = lax.all_gather(first, "fsdp", axis=0, tiled=True)
    wqkv = first[:, : 3 * span]
    wup = jnp.concatenate([columns(w_up, f * units + me * part, part) for f in range(owners)], axis=1)
    wdown = lax.dynamic_slice_in_dim(w_down, me * part, part, 0)
    if part == depth:
        second = lax.all_gather(jnp.concatenate([wup, wdown], axis=1), "fsdp", axis=0, tiled=True)
        wup, wdown = second[:, :ff], second[:, ff:]
    else:
        wup = lax.all_gather(wup, "fsdp", axis=0, tiled=True)
        wdown = lax.all_gather(wdown, "fsdp", axis=0, tiled=True)

    states = []
    for c in range(clips):
        piece = frames_in[c]
        if states:
            piece = lax.optimization_barrier((piece, states[-1][0][-1]))[0]
        states.append(gather_begin(piece))

    packed = jnp.concatenate(
        [norm1_gain, norm1_bias, query_bias, value_bias, attn_out_bias, norm2_gain, norm2_bias,
         down_bias, up_bias]
    )[None]
    vectors = jnp.stack(butterfly(packed)).astype(single)

    def vector(k):
        return vectors[:, k * depth : (k + 1) * depth].reshape(1, width)

    gain1, bias1, qbias, vbias, obias, gain2, bias2, dbias = (vector(k) for k in range(8))
    ubias = lax.dynamic_slice_in_dim(vectors, 8 * depth + me * part, part, 1).reshape(1, ff)
    qkv_bias = jnp.concatenate(
        [columns(qbias, me * span, span), jnp.zeros((1, span), single), columns(vbias, me * span, span)],
        axis=1,
    )

    quarters = gather_all(first[:, 3 * span :])

    mine = lax.dynamic_slice_in_dim(lengths, own * clips, clips)
    order = (me ^ jnp.arange(groups, dtype=jnp.int32))[:, None] * frames + jnp.arange(
        frames, dtype=jnp.int32
    )
    order = order.reshape(seq_len)
    count = jnp.sum(lengths).astype(single)
    lane0 = (jnp.arange(LANES - dim) == 0)[None, :]
    masks = [
        jnp.where((order >= mine[c])[:, None] & lane0, -1e30, 0.0).astype(half) for c in range(clips)
    ]
    row_valid = [(order[:frames] < mine[c]).astype(single)[:, None] for c in range(clips)]

    step = Order()

    n = frames
    every = range(clips)
    full1 = [None] * clips
    qkvs, sums, moved, contexts = ([None] * clips for _ in range(4))
    middles, hiddens, actives, slopes, branches = ([None] * clips for _ in range(5))
    outs, losses, grad_outs, pieces = ([None] * clips for _ in range(4))
    grad_uppers, grad_hidden2, grad_middles, grad_branches = ([None] * clips for _ in range(4))
    grad_heads, grad_qkvs, grad_hidden1, grads_in = ([None] * clips for _ in range(4))
    stats2 = [None] * clips
    norm2_grads, norm1_grads = [None] * clips, [None] * clips

    def rows_of(array, r):
        return array[r * n : (r + 1) * n]

    def owned(grad):
        return lax.psum_scatter(grad, "fsdp", scatter_dimension=0, tiled=True)

    def arriving(store, c):
        near, far = store[c]
        yield from near
        far = gather_end(step.after(far))
        store[c] = near + far
        yield from far

    def norm1(c):
        near, far = states[c]
        full1[c] = norm_blocks(near + gather_end(step.after(far)), gain1, bias1)
        step.mark(full1[c])

    def attention(c):
        qkvs[c] = (dot(step.after(full1[c]), wqkv) + qkv_bias).astype(half)
        context, sums[c] = attend(qkvs[c], masks[c], heads, dim, scale)
        parts = [rows_of(context, r) for r in range(groups)]
        step.mark(*parts)
        moved[c] = swap(parts)

    def project(c):
        contexts[c] = jnp.concatenate(moved[c][:1] + step.after_all(moved[c][1:]), axis=1)
        middles[c] = frames_in[c].astype(single) + dot(contexts[c], wout) + obias
        stats2[c] = norm_stats(middles[c])
        hidden = layer_norm(middles[c], stats2[c], gain2, bias2).astype(half)
        step.mark(hidden)
        hiddens[c] = gather_begin(hidden)

    def feed_forward(c):
        near, far = hiddens[c]
        hiddens[c] = near + gather_end(step.after(far))
        actives[c], slopes[c] = [None] * groups, [None] * groups

        def term(r):
            upper = dot(step.after(hiddens[c][r]), wup) + ubias
            cdf = 0.5 * (1.0 + lax.erf(upper * math.sqrt(0.5)))
            actives[c][r] = (upper * cdf).astype(half)
            slopes[c][r] = (
                cdf + upper * (jnp.exp(-0.5 * upper * upper) * (1.0 / math.sqrt(2.0 * math.pi)))
            ).astype(half)
            step.mark(actives[c][r])
            return marked(dot(step.after(actives[c][r]), wdown).astype(half))

        branches[c] = scatter_terms(term, step)

    def loss(c):
        branch = add_terms(branches[c][:1] + step.after_all(branches[c][1:]))
        result = middles[c] + branch + dbias
        outs[c] = result.astype(half)
        diff = result - teacher[c].astype(single)
        masked = diff * row_valid[c]
        losses[c] = jnp.sum(masked * diff) / (2.0 * width * count)
        grad_outs[c] = masked * (float(lengths.shape[0] * seq_len) / count)
        branch = grad_outs[c].astype(half)
        step.mark(branch)
        pieces[c] = gather_begin(branch)

    def back_up(c):
        grad_uppers[c] = []
        for block in arriving(pieces, c):
            grad = dot_t(step.after(block), wdown) * slopes[c][len(grad_uppers[c])].astype(single)
            grad_uppers[c].append(grad.astype(half))
            step.mark(grad_uppers[c][-1])

    def back_down(c):
        grad_hidden2[c] = scatter_terms(
            lambda r: marked(dot_t(step.after(grad_uppers[c][r]), wup).astype(half)), step
        )

    def norm2(c):
        grad = add_terms(grad_hidden2[c][:1] + step.after_all(grad_hidden2[c][1:]))
        gm, *norm2_grads[c] = norm_back(middles[c], stats2[c], gain2, grad)
        grad_middles[c] = grad_outs[c] + gm
        grad_branches[c] = grad_middles[c].astype(half)
        grad_context = dot_t(grad_branches[c], wout).astype(half)
        parts = [grad_context[:, r * span : (r + 1) * span] for r in range(groups)]
        step.mark(*parts)
        grad_heads[c] = swap(parts)

    def attention_back(c):
        grad_head = jnp.concatenate(grad_heads[c][:1] + step.after_all(grad_heads[c][1:]), axis=0)
        grad_qkvs[c] = attend_back(qkvs[c], masks[c], grad_head, sums[c], heads, dim, scale)
        step.mark(grad_qkvs[c])

    def marked(tensor):
        step.mark(tensor)
        return tensor

    def hidden_back(c):
        found = spread_terms(step.after(grad_qkvs[c]), wqkv, groups)
        step.mark(*found)
        grad_hidden1[c] = scatter_terms(lambda r: found[r], step)

    def norm1_back(c):
        state = frames_in[c].astype(single)
        grad = add_terms(grad_hidden1[c][:1] + step.after_all(grad_hidden1[c][1:]))
        gs, *norm1_grads[c] = norm_back(state, norm_stats(state), gain1, grad)
        grads_in[c] = grad_middles[c] + gs
        step.mark(grads_in[c])

    first_clip, *others = every
    for c in every:
        norm1(c)
    attention(first_clip)
    wout = arrange(
        gather_blocks_kernel, quarters, jax.ShapeDtypeStruct((width, width), half), groups, me,
        "place_output_weight",
    )
    for c in others:
        attention(c)
    for c in every:
        project(c)
    for c in every:
        feed_forward(c)
    for c in every:
        loss(c)
    for c in every:
        back_up(c)
        back_down(c)

    def flat(store):
        return [x for blocks in store for x in blocks]

    def ordered(lefts):
        return [step.after(lefts[0])] + lefts[1:]

    joined = part == depth
    norm2(first_clip)
    grad_wdown = products(ordered(flat(actives)), flat(pieces), half, slots=1 + joined)
    step.mark(grad_wdown)
    grad_wup = products(
        ordered(flat(hiddens)), flat(grad_uppers), half,
        **(dict(into=grad_wdown, slot=1, slots=2) if joined else {}),
    )
    step.mark(grad_wup)
    if joined:
        both = owned(grad_wup)
        grad_wdown, grad_wup = both[:, :width], both[:, width:]
    else:
        grad_wdown, grad_wup = owned(grad_wdown), owned(grad_wup)
    for c in others:
        norm2(c)
    grad_wout = products(ordered(contexts), grad_branches, half)
    step.mark(grad_wout)
    quarters = arrange(
        scatter_blocks_kernel, [grad_wout],
        [jax.ShapeDtypeStruct((width, -(-span // LANES) * LANES), half)] * groups, groups, me,
        "split_output_weight",
    )
    attention_back(first_clip)
    grad_wout = scatter_terms(lambda r: quarters[r], Order())
    grad_wout = add_terms([step.after(grad_wout[0])] + grad_wout[1:]).astype(half)
    step.mark(grad_wout)
    for c in others:
        attention_back(c)
    step.also(grad_wup)
    total = products(ordered(full1), grad_qkvs, half, beside=grad_wout, width=span)
    step.mark(total)
    total = owned(total)
    for c in every:
        hidden_back(c)
    for c in every:
        norm1_back(c)
    grad_wdown, grad_wup = (gather_all(g) for g in step.after_all([grad_wdown, grad_wup]))
    late = step.after_all(grad_qkvs)
    frames_out = jnp.stack(outs)
    grad_gain1, grad_bias1 = (sum(g) for g in zip(*norm1_grads))
    grad_gain2, grad_bias2 = (sum(g) for g in zip(*norm2_grads))
    grad_dbias = sum(jnp.sum(g.astype(half).astype(single), axis=0) for g in grad_outs)
    grad_ubias = sum(jnp.sum(g.astype(single), axis=0) for blocks in grad_uppers for g in blocks)
    grad_obias = sum(jnp.sum(g.astype(single), axis=0) for g in grad_branches)
    grad_qkv_bias = sum(jnp.sum(g.astype(single), axis=0) for g in late)

    def rows8(v):
        return v.reshape(owners, depth)

    def spread(v):
        return lax.dynamic_update_slice(jnp.zeros((width,), single), v, (me * span,))

    slot = (jnp.arange(groups) == me).astype(single)[None, :, None]
    rows = jnp.concatenate(
        [rows8(grad_gain1), rows8(grad_bias1), rows8(spread(grad_qkv_bias[:span])),
         rows8(spread(grad_qkv_bias[2 * span :])), rows8(grad_obias), rows8(grad_gain2),
         rows8(grad_bias2), rows8(grad_dbias),
         (grad_ubias.reshape(owners, 1, part) * slot).reshape(owners, units)],
        axis=1,
    )
    rows = jnp.take(rows, own ^ jnp.arange(owners), axis=0)
    bits = owners // 2
    while bits:
        rows = rows[:bits] + flip(rows[bits:], bits, "fsdp")
        bits //= 2
    rows = jnp.concatenate([rows[0], jnp.stack(losses)])
    bits = 1
    while bits < groups:
        rows = rows + flip(rows, bits)
        bits *= 2
    step.mark(rows)
    small = [rows[k * depth : (k + 1) * depth] for k in range(8)]
    small_up = rows[8 * depth : 8 * depth + units]
    clip_loss = rows[8 * depth + units :]

    total = step.after(total)
    pieces_last = gather_all(total)
    step.mark(total)
    grad_in = jnp.stack(step.after_all(grads_in))
    grad_wdown = assemble(step.after_all(grad_wdown), 0, me)
    grad_wup = assemble(step.after_all(grad_wup), owners, me)
    step.mark(grad_in, grad_wdown, grad_wup)
    pieces_last = pieces_last[:1] + step.after_all(pieces_last[1:])
    grad_wqkv = assemble(pieces_last, 3, me, 0, 3 * span)
    grad_wout = assemble(pieces_last, 1, me, 3 * span, span)
    return (
        frames_out, clip_loss, grad_in, small[0], small[1], grad_wqkv, small[2], small[3],
        grad_wout, small[4], small[5], small[6], grad_wup, small_up, grad_wdown, small[7],
    )


def solution(mesh):
    vec, mat, act = P("fsdp"), P("fsdp", None), P("fsdp", "seq", None)
    return jax.shard_map(
        local,
        mesh=mesh,
        in_specs=(act, act, P(), vec, vec, mat, vec, vec, mat, vec, vec, vec, mat, vec, mat, vec),
        out_specs=(act, vec, act, vec, vec, mat, vec, vec, mat, vec, vec, vec, mat, vec, mat, vec),
        check_vma=False,
    )
```

```python
import functools
import math

import jax
import jax.numpy as jnp
from jax import lax
from jax.experimental import pallas as pl
from jax.experimental.pallas import tpu as pltpu
from jax.sharding import PartitionSpec as P

HEADS = 16
LANES = 128
LOG2E = 1.0 / math.log(2.0)
single = jnp.float32
half = jnp.bfloat16


def norm_stats(v):
    mean = jnp.mean(v, axis=-1, keepdims=True)
    cent = v - mean
    var = jnp.mean(cent * cent, axis=-1, keepdims=True)
    return mean, lax.rsqrt(var + 1e-05)


def layer_norm(v, stats, gain, bias):
    return (v - stats[0]) * stats[1] * gain + bias


def norm_back(v, stats, gain, grad):
    scaled = (v - stats[0]) * stats[1]
    inner = grad * gain
    first = jnp.mean(inner, axis=-1, keepdims=True)
    second = jnp.mean(inner * scaled, axis=-1, keepdims=True)
    return (
        stats[1] * (inner - first - scaled * second),
        jnp.sum(grad * scaled, axis=0),
        jnp.sum(grad, axis=0),
    )


def flip(tensor, bits, axis="seq"):
    return lax.ppermute(
        tensor, axis, [(i, i ^ bits) for i in range(lax.axis_size(axis))]
    )


def gather_low(piece, size):
    blocks = {0: piece}
    bits = size // 2
    while bits:
        for r in sorted(blocks):
            blocks[r | bits] = flip(blocks[r], bits)
        bits //= 2
    return [blocks[r] for r in range(size)]


def gather_begin(piece):
    size = lax.axis_size("seq") // 2
    far = flip(piece, size)
    return gather_low(piece, size), far


def gather_end(far):
    return gather_low(far, lax.axis_size("seq") // 2)


def gather_all(piece):
    near, far = gather_begin(piece)
    return near + gather_end(far)


def scatter_terms(make, step):
    groups = lax.axis_size("seq")

    def terms(base, size):
        if size == 1:
            out = make(base)
            step.mark(out)
            return [out]
        near = size // 2
        high = terms(base + near, near)
        if len(high) > 1:
            high = step.after(high[0]).astype(single) + sum(h.astype(single) for h in high[1:])
            high = high.astype(half)
            step.mark(high)
        else:
            high = high[0]
        moved = flip(high, near)
        return terms(base, near) + [moved]

    return terms(0, groups)


def add_terms(parts):
    return sum(p.astype(single) for p in parts)


def swap(parts):
    return [parts[0]] + [flip(parts[r], r) for r in range(1, len(parts))]


def pad_lanes(tensor, tail):
    return jnp.concatenate([tensor, tail], axis=1)


def unit_tail(rows, width):
    lane = lax.broadcasted_iota(jnp.int32, (rows, width), 1)
    return jnp.where(lane == 0, 1.0, 0.0).astype(half)


def attend_kernel(heads, dim, block, scale, qkv_ref, mask_ref, ctx_ref, lse_ref, keys, values):
    seq = qkv_ref.shape[0]
    span = heads * dim
    rest = LANES - dim
    rate = scale * LOG2E
    for j in range(heads):
        keys[j] = pad_lanes(
            qkv_ref[:, span + j * dim : span + (j + 1) * dim], mask_ref[...]
        )
        values[j] = pad_lanes(
            qkv_ref[:, 2 * span + j * dim : 2 * span + (j + 1) * dim], unit_tail(seq, rest)
        )

    def one_block(i, carry):
        rows = pl.ds(pl.multiple_of(i * block, block), block)
        ones = unit_tail(block, rest)
        contexts, sums = [], []
        for j in range(heads):
            query = pad_lanes(qkv_ref[rows, j * dim : (j + 1) * dim], ones)
            scores = lax.dot_general(
                query, keys[j], (((1,), (1,)), ((), ())), preferred_element_type=single
            )
            top = jnp.max(scores, axis=-1, keepdims=True) * rate
            probs = jnp.exp2(scores * rate - top).astype(half)
            mixed = jnp.dot(probs, values[j], preferred_element_type=single)
            total = mixed[:, dim : dim + 1]
            contexts.append((mixed[:, :dim] / total).astype(half))
            sums.append(top + jnp.log(total) * LOG2E)
        ctx_ref[rows, :] = jnp.concatenate(contexts, axis=1)
        lse_ref[rows, :] = jnp.concatenate(sums, axis=1)
        return carry

    lax.fori_loop(0, seq // block, one_block, 0)


def attend_back_kernel(
    heads, dim, block, scale,
    qkv_ref, mask_ref, grad_ref, lse_ref, out_ref, keys, values, gkeys, gvalues, gquery,
):
    seq = qkv_ref.shape[0]
    span = heads * dim
    rest = LANES - dim
    rate = scale * LOG2E
    for j in range(heads):
        keys[j] = pad_lanes(
            qkv_ref[:, span + j * dim : span + (j + 1) * dim], mask_ref[...]
        )
        values[j] = pad_lanes(
            qkv_ref[:, 2 * span + j * dim : 2 * span + (j + 1) * dim],
            jnp.zeros((seq, rest), half),
        )
    gkeys[...] = jnp.zeros_like(gkeys)
    gvalues[...] = jnp.zeros_like(gvalues)

    def one_block(i, carry):
        rows = pl.ds(pl.multiple_of(i * block, block), block)
        ones = unit_tail(block, rest)
        none = jnp.zeros((block, rest), half)
        pieces = []
        for j in range(heads):
            query = pad_lanes(qkv_ref[rows, j * dim : (j + 1) * dim], ones)
            grad = pad_lanes(grad_ref[rows, j * dim : (j + 1) * dim], none)
            scores = lax.dot_general(
                query, keys[j], (((1,), (1,)), ((), ())), preferred_element_type=single
            )
            probs = jnp.exp2(scores * rate - lse_ref[rows, j : j + 1])
            dprobs = lax.dot_general(
                grad, values[j], (((1,), (1,)), ((), ())), preferred_element_type=single
            )
            inner = jnp.sum(probs * dprobs, axis=-1, keepdims=True)
            dscores = (probs * (dprobs - inner)).astype(half)
            pieces.append(
                (jnp.dot(dscores, keys[j], preferred_element_type=single)[:, :dim] * scale).astype(half)
            )
            gkeys[j] += jnp.dot(query.T, dscores, preferred_element_type=single)
            gvalues[j] += jnp.dot(grad.T, probs.astype(half), preferred_element_type=single)
        gquery[rows, :] = jnp.concatenate(pieces, axis=1)
        return carry

    lax.fori_loop(0, seq // block, one_block, 0)

    def put(i, carry):
        rows = pl.ds(pl.multiple_of(i * block, block), block)
        pieces = [gquery[rows, :]]
        for j in range(heads):
            pieces.append((gkeys[j, :, rows].T[:, :dim] * scale).astype(half))
        for j in range(heads):
            pieces.append(gvalues[j, :, rows].T[:, :dim].astype(half))
        out_ref[rows, :] = jnp.concatenate(pieces, axis=1)
        return carry

    lax.fori_loop(0, seq // block, put, 0)


def attend(qkv, mask, heads, dim, scale):
    seq = qkv.shape[0]
    block = next(b for b in (768, 512, 256, seq) if seq % b == 0)
    return pl.pallas_call(
        functools.partial(attend_kernel, heads, dim, block, scale),
        out_shape=(
            jax.ShapeDtypeStruct((seq, heads * dim), half),
            jax.ShapeDtypeStruct((seq, heads), single),
        ),
        scratch_shapes=[
            pltpu.VMEM((heads, seq, LANES), half),
            pltpu.VMEM((heads, seq, LANES), half),
        ],
        compiler_params=pltpu.CompilerParams(vmem_limit_bytes=48 << 20),
        cost_estimate=pl.CostEstimate(
            flops=4 * heads * seq * seq * 256, bytes_accessed=qkv.size * 3, transcendentals=heads * seq * seq
        ),
        name="attend",
    )(qkv, mask)


def attend_back(qkv, mask, grad, lse, heads, dim, scale):
    seq = qkv.shape[0]
    block = next(b for b in (768, 512, 256, seq) if seq % b == 0)
    return pl.pallas_call(
        functools.partial(attend_back_kernel, heads, dim, block, scale),
        out_shape=jax.ShapeDtypeStruct(qkv.shape, half),
        scratch_shapes=[
            pltpu.VMEM((heads, seq, LANES), half),
            pltpu.VMEM((heads, seq, LANES), half),
            pltpu.VMEM((heads, LANES, seq), single),
            pltpu.VMEM((heads, LANES, seq), single),
            pltpu.VMEM((seq, heads * dim), half),
        ],
        compiler_params=pltpu.CompilerParams(vmem_limit_bytes=56 << 20),
        cost_estimate=pl.CostEstimate(
            flops=20 * heads * seq * seq * 256, bytes_accessed=qkv.size * 5, transcendentals=heads * seq * seq
        ),
        name="attend_back",
    )(qkv, mask, grad, lse)


def norm_kernel(groups, chunk, *refs):
    blocks, gain_ref, bias_ref, out = refs[:groups], refs[groups], refs[groups + 1], refs[groups + 2]
    rows = blocks[0].shape[0]
    for r in range(groups):

        def some(i, carry, r=r):
            start = pl.multiple_of(i * chunk, chunk)
            v = blocks[r][pl.ds(start, chunk), :].astype(single)
            out[pl.ds(r * rows + start, chunk), :] = layer_norm(v, norm_stats(v), gain_ref[...], bias_ref[...]).astype(
                half
            )
            return carry

        lax.fori_loop(0, rows // chunk, some, 0)


def norm_blocks(blocks, gain, bias):
    groups = len(blocks)
    rows, width = blocks[0].shape
    return pl.pallas_call(
        functools.partial(norm_kernel, groups, 64 if rows % 128 else 128),
        out_shape=jax.ShapeDtypeStruct((groups * rows, width), half),
        cost_estimate=pl.CostEstimate(
            flops=groups * rows * width * 10, bytes_accessed=groups * rows * width * 4, transcendentals=0
        ),
        name="norm_blocks",
    )(*blocks, gain, bias)


def products_kernel(pairs, before, beside, *refs):
    lefts, rights = refs[:pairs], refs[pairs : 2 * pairs]
    more, out = refs[2 * pairs : -1], refs[-1]
    total = more[0][...] if before else None
    for a, b in zip(lefts, rights):
        term = lax.dot_general(
            a[...], b[...], (((0,), (0,)), ((), ())), preferred_element_type=single
        )
        total = term if total is None else total + term
    total = total.astype(out.dtype)
    if beside:
        total = jnp.concatenate([total, more[-1][:, :beside]], axis=1)
    out[...] = total


def products(lefts, rights, kind, before=None, beside=None, width=0, into=None, slot=0, slots=1):
    pairs = len(lefts)
    rows, cols = lefts[0].shape[1], rights[0].shape[1]
    tile = next(t for t in (256, 128, rows) if rows % t == 0)
    depth = sum(a.shape[0] for a in lefts)
    in_specs = [pl.BlockSpec((a.shape[0], tile), lambda i: (0, i)) for a in lefts]
    in_specs += [pl.BlockSpec(b.shape, lambda i: (0, 0)) for b in rights]
    more = []
    if before is not None:
        more.append(before)
        in_specs.append(pl.BlockSpec((tile, cols), lambda i: (i, 0)))
    if beside is not None:
        more.append(beside)
        in_specs.append(pl.BlockSpec((tile, beside.shape[1]), lambda i: (i, 0)))
        cols += width
    body = functools.partial(products_kernel, pairs, before is not None, width)
    aliases = {}
    if into is not None:
        aliases = {2 * pairs + len(more): 0}
        more.append(into)
        in_specs.append(pl.BlockSpec(memory_space=pl.ANY))
        inner = body

        def body(*refs):
            inner(*refs[:-2], refs[-1])

    return pl.pallas_call(
        body,
        grid=(rows // tile,),
        in_specs=in_specs,
        out_specs=pl.BlockSpec((tile, cols), lambda i: (i, slot)),
        out_shape=jax.ShapeDtypeStruct((rows, cols * slots), kind),
        input_output_aliases=aliases,
        compiler_params=pltpu.CompilerParams(vmem_limit_bytes=56 << 20),
        cost_estimate=pl.CostEstimate(
            flops=2 * depth * rows * cols, bytes_accessed=2 * depth * (rows + cols), transcendentals=0
        ),
        name="products",
    )(*lefts, *rights, *more)


def spread_kernel(grad, weight, *outs):
    n = outs[0].shape[0]
    for r, out in enumerate(outs):
        out[...] = lax.dot_general(
            grad[r * n : (r + 1) * n, :], weight[...], (((1,), (1,)), ((), ())),
            preferred_element_type=single,
        ).astype(half)


def spread_terms(grad, weight, groups):
    rows, cols = grad.shape[0] // groups, weight.shape[0]
    return pl.pallas_call(
        spread_kernel,
        out_shape=[jax.ShapeDtypeStruct((rows, cols), half)] * groups,
        compiler_params=pltpu.CompilerParams(vmem_limit_bytes=32 << 20),
        cost_estimate=pl.CostEstimate(flops=0, bytes_accessed=0, transcendentals=0),
        name="spread_terms",
    )(grad, weight)


def assemble_kernel(groups, counts, width, start, me_ref, *refs):
    pieces, out = refs[:groups], refs[groups]
    rows = pieces[0].shape[0]
    for v in range(groups):

        @pl.when(me_ref[0] == v)
        def _():
            for g in range(groups):
                piece = pieces[v ^ g]
                if counts == 0:
                    out[g * rows : (g + 1) * rows, :] = piece[...].astype(single)
            if counts:
                blocks = [
                    pieces[v ^ g][:, start + k * width : start + (k + 1) * width]
                    for k in range(counts)
                    for g in range(groups)
                ]
                out[...] = jnp.concatenate(blocks, axis=1).astype(single)


def assemble(pieces, counts, me, start=0, cols=None):
    groups = len(pieces)
    rows = pieces[0].shape[0]
    cols = cols or pieces[0].shape[1]
    shape = (rows, cols * groups) if counts else (rows * groups, cols)
    return pl.pallas_call(
        functools.partial(assemble_kernel, groups, counts, cols // max(counts, 1), start),
        out_shape=jax.ShapeDtypeStruct(shape, single),
        in_specs=[pl.BlockSpec(memory_space=pltpu.SMEM)]
        + [pl.BlockSpec(memory_space=pltpu.VMEM)] * groups,
        cost_estimate=pl.CostEstimate(
            flops=0, bytes_accessed=rows * cols * groups * 6, transcendentals=0
        ),
        name="assemble",
    )(me.astype(jnp.int32).reshape(1), *pieces)


def gather_blocks_kernel(groups, me_ref, *refs):
    pieces, out = refs[:groups], refs[groups]
    span = pieces[0].shape[1]
    for v in range(groups):

        @pl.when(me_ref[0] == v)
        def _():
            for r in range(groups):
                rows = [
                    pieces[v ^ g][(v ^ r) * span : ((v ^ r) + 1) * span, :] for g in range(groups)
                ]
                out[r * span : (r + 1) * span, :] = jnp.concatenate(rows, axis=1)


def scatter_blocks_kernel(groups, me_ref, full, *outs):
    span = full.shape[1] // groups
    spare = outs[0].shape[1] - span
    for v in range(groups):

        @pl.when(me_ref[0] == v)
        def _():
            for r in range(groups):
                for g in range(groups):
                    block = full[
                        (v ^ g) * span : ((v ^ g) + 1) * span, (v ^ r) * span : ((v ^ r) + 1) * span
                    ]
                    if spare:
                        block = jnp.concatenate([block, jnp.zeros((span, spare), block.dtype)], axis=1)
                    outs[r][g * span : (g + 1) * span, :] = block


def arrange(kernel, arrays, shapes, groups, me, name):
    return pl.pallas_call(
        functools.partial(kernel, groups),
        out_shape=shapes,
        in_specs=[pl.BlockSpec(memory_space=pltpu.SMEM)]
        + [pl.BlockSpec(memory_space=pltpu.VMEM)] * len(arrays),
        cost_estimate=pl.CostEstimate(
            flops=0, bytes_accessed=sum(x.size for x in arrays) * 4, transcendentals=0
        ),
        name=name,
    )(me.astype(jnp.int32).reshape(1), *arrays)


class Order:
    def __init__(self):
        self.tokens = []

    def after(self, tensor):
        if not self.tokens:
            return tensor
        return lax.optimization_barrier((tensor, *self.tokens))[0]

    def after_all(self, tensors):
        return list(lax.optimization_barrier((*tensors, *self.tokens))[: len(tensors)])

    def mark(self, *tensors):
        self.tokens = list(tensors)

    def also(self, *tensors):
        self.tokens += tensors


def local(
    frames_in, teacher, lengths, norm1_gain, norm1_bias, w_qkv, query_bias, value_bias,
    w_attn_out, attn_out_bias, norm2_gain, norm2_bias, w_up, up_bias, w_down, down_bias,
):
    clips, frames, width = frames_in.shape
    groups = lax.axis_size("seq")
    owners = lax.axis_size("fsdp")
    me = lax.axis_index("seq")
    own = lax.axis_index("fsdp")
    seq_len = frames * groups
    dim = width // HEADS
    heads = HEADS // groups
    span = heads * dim
    depth = w_qkv.shape[0]
    units = w_down.shape[0]
    part = units // groups
    scale = 1.0 / math.sqrt(dim)

    def dot(a, b):
        return jnp.dot(a, b, preferred_element_type=single)

    def dot_t(a, b):
        return lax.dot_general(a, b, (((1,), (1,)), ((), ())), preferred_element_type=single)

    def t_dot(a, b):
        return lax.dot_general(a, b, (((0,), (0,)), ((), ())), preferred_element_type=single)

    def columns(array, start, size):
        return lax.dynamic_slice_in_dim(array, start, size, 1)

    def butterfly(array):
        bits = 1
        while bits < owners:
            array = jnp.concatenate([array, flip(array, bits, "fsdp")], axis=0)
            bits *= 2
        return [
            lax.dynamic_index_in_dim(array, own ^ f, 0, keepdims=False) for f in range(owners)
        ]

    ff = owners * part
    first = jnp.concatenate(
        [columns(w_qkv, k * width + me * span, span) for k in range(3)]
        + [columns(w_attn_out, me * span, span)],
        axis=1,
    )
    first = lax.all_gather(first, "fsdp", axis=0, tiled=True)
    wqkv = first[:, : 3 * span]
    wup = jnp.concatenate([columns(w_up, f * units + me * part, part) for f in range(owners)], axis=1)
    wdown = lax.dynamic_slice_in_dim(w_down, me * part, part, 0)
    if part == depth:
        second = lax.all_gather(jnp.concatenate([wup, wdown], axis=1), "fsdp", axis=0, tiled=True)
        wup, wdown = second[:, :ff], second[:, ff:]
    else:
        wup = lax.all_gather(wup, "fsdp", axis=0, tiled=True)
        wdown = lax.all_gather(wdown, "fsdp", axis=0, tiled=True)

    states = []
    for c in range(clips):
        piece = frames_in[c]
        if states:
            piece = lax.optimization_barrier((piece, states[-1][0][-1]))[0]
        states.append(gather_begin(piece))

    packed = jnp.concatenate(
        [norm1_gain, norm1_bias, query_bias, value_bias, attn_out_bias, norm2_gain, norm2_bias,
         down_bias, up_bias]
    )[None]
    vectors = jnp.stack(butterfly(packed)).astype(single)

    def vector(k):
        return vectors[:, k * depth : (k + 1) * depth].reshape(1, width)

    gain1, bias1, qbias, vbias, obias, gain2, bias2, dbias = (vector(k) for k in range(8))
    ubias = lax.dynamic_slice_in_dim(vectors, 8 * depth + me * part, part, 1).reshape(1, ff)
    qkv_bias = jnp.concatenate(
        [columns(qbias, me * span, span), jnp.zeros((1, span), single), columns(vbias, me * span, span)],
        axis=1,
    )

    quarters = gather_all(first[:, 3 * span :])

    mine = lax.dynamic_slice_in_dim(lengths, own * clips, clips)
    order = (me ^ jnp.arange(groups, dtype=jnp.int32))[:, None] * frames + jnp.arange(
        frames, dtype=jnp.int32
    )
    order = order.reshape(seq_len)
    count = jnp.sum(lengths).astype(single)
    lane0 = (jnp.arange(LANES - dim) == 0)[None, :]
    masks = [
        jnp.where((order >= mine[c])[:, None] & lane0, -1e30, 0.0).astype(half) for c in range(clips)
    ]
    row_valid = [(order[:frames] < mine[c]).astype(single)[:, None] for c in range(clips)]

    step = Order()

    n = frames
    every = range(clips)
    full1 = [None] * clips
    qkvs, sums, moved, contexts = ([None] * clips for _ in range(4))
    middles, hiddens, actives, slopes, branches = ([None] * clips for _ in range(5))
    outs, losses, grad_outs, pieces = ([None] * clips for _ in range(4))
    grad_uppers, grad_hidden2, grad_middles, grad_branches = ([None] * clips for _ in range(4))
    grad_heads, grad_qkvs, grad_hidden1, grads_in = ([None] * clips for _ in range(4))
    stats2 = [None] * clips
    norm2_grads, norm1_grads = [None] * clips, [None] * clips

    def rows_of(array, r):
        return array[r * n : (r + 1) * n]

    def owned(grad):
        return lax.psum_scatter(grad, "fsdp", scatter_dimension=0, tiled=True)

    def arriving(store, c):
        near, far = store[c]
        yield from near
        far = gather_end(step.after(far))
        store[c] = near + far
        yield from far

    def norm1(c):
        near, far = states[c]
        full1[c] = norm_blocks(near + gather_end(step.after(far)), gain1, bias1)
        step.mark(full1[c])

    def attention(c):
        qkvs[c] = (dot(step.after(full1[c]), wqkv) + qkv_bias).astype(half)
        context, sums[c] = attend(qkvs[c], masks[c], heads, dim, scale)
        parts = [rows_of(context, r) for r in range(groups)]
        step.mark(*parts)
        moved[c] = swap(parts)

    def project(c):
        contexts[c] = jnp.concatenate(moved[c][:1] + step.after_all(moved[c][1:]), axis=1)
        middles[c] = frames_in[c].astype(single) + dot(contexts[c], wout) + obias
        stats2[c] = norm_stats(middles[c])
        hidden = layer_norm(middles[c], stats2[c], gain2, bias2).astype(half)
        step.mark(hidden)
        hiddens[c] = gather_begin(hidden)

    def feed_forward(c):
        near, far = hiddens[c]
        hiddens[c] = near + gather_end(step.after(far))
        actives[c], slopes[c] = [None] * groups, [None] * groups

        def term(r):
            upper = dot(step.after(hiddens[c][r]), wup) + ubias
            cdf = 0.5 * (1.0 + lax.erf(upper * math.sqrt(0.5)))
            actives[c][r] = (upper * cdf).astype(half)
            slopes[c][r] = (
                cdf + upper * (jnp.exp(-0.5 * upper * upper) * (1.0 / math.sqrt(2.0 * math.pi)))
            ).astype(half)
            step.mark(actives[c][r])
            return marked(dot(step.after(actives[c][r]), wdown).astype(half))

        branches[c] = scatter_terms(term, step)

    def loss(c):
        branch = add_terms(branches[c][:1] + step.after_all(branches[c][1:]))
        result = middles[c] + branch + dbias
        outs[c] = result.astype(half)
        diff = result - teacher[c].astype(single)
        masked = diff * row_valid[c]
        losses[c] = jnp.sum(masked * diff) / (2.0 * width * count)
        grad_outs[c] = masked * (float(lengths.shape[0] * seq_len) / count)
        branch = grad_outs[c].astype(half)
        step.mark(branch)
        pieces[c] = gather_begin(branch)

    def back_up(c):
        grad_uppers[c] = []
        for block in arriving(pieces, c):
            grad = dot_t(step.after(block), wdown) * slopes[c][len(grad_uppers[c])].astype(single)
            grad_uppers[c].append(grad.astype(half))
            step.mark(grad_uppers[c][-1])

    def back_down(c):
        grad_hidden2[c] = scatter_terms(
            lambda r: marked(dot_t(step.after(grad_uppers[c][r]), wup).astype(half)), step
        )

    def norm2(c):
        grad = add_terms(grad_hidden2[c][:1] + step.after_all(grad_hidden2[c][1:]))
        gm, *norm2_grads[c] = norm_back(middles[c], stats2[c], gain2, grad)
        grad_middles[c] = grad_outs[c] + gm
        grad_branches[c] = grad_middles[c].astype(half)
        grad_context = dot_t(grad_branches[c], wout).astype(half)
        parts = [grad_context[:, r * span : (r + 1) * span] for r in range(groups)]
        step.mark(*parts)
        grad_heads[c] = swap(parts)

    def attention_back(c):
        grad_head = jnp.concatenate(grad_heads[c][:1] + step.after_all(grad_heads[c][1:]), axis=0)
        grad_qkvs[c] = attend_back(qkvs[c], masks[c], grad_head, sums[c], heads, dim, scale)
        step.mark(grad_qkvs[c])

    def marked(tensor):
        step.mark(tensor)
        return tensor

    def hidden_back(c):
        found = spread_terms(step.after(grad_qkvs[c]), wqkv, groups)
        step.mark(*found)
        grad_hidden1[c] = scatter_terms(lambda r: found[r], step)

    def norm1_back(c):
        state = frames_in[c].astype(single)
        grad = add_terms(grad_hidden1[c][:1] + step.after_all(grad_hidden1[c][1:]))
        gs, *norm1_grads[c] = norm_back(state, norm_stats(state), gain1, grad)
        grads_in[c] = grad_middles[c] + gs
        step.mark(grads_in[c])

    first_clip, *others = every
    for c in every:
        norm1(c)
    attention(first_clip)
    wout = arrange(
        gather_blocks_kernel, quarters, jax.ShapeDtypeStruct((width, width), half), groups, me,
        "place_output_weight",
    )
    for c in others:
        attention(c)
    for c in every:
        project(c)
    for c in every:
        feed_forward(c)
    for c in every:
        loss(c)
    for c in every:
        back_up(c)
        back_down(c)

    def flat(store):
        return [x for blocks in store for x in blocks]

    def ordered(lefts):
        return [step.after(lefts[0])] + lefts[1:]

    joined = part == depth
    grad_wdown = products(ordered(flat(actives)), flat(pieces), half, slots=1 + joined)
    step.mark(grad_wdown)
    norm2(first_clip)
    grad_wup = products(
        ordered(flat(hiddens)), flat(grad_uppers), half,
        **(dict(into=grad_wdown, slot=1, slots=2) if joined else {}),
    )
    step.mark(grad_wup)
    if joined:
        both = owned(grad_wup)
        grad_wdown, grad_wup = both[:, :width], both[:, width:]
    else:
        grad_wdown, grad_wup = owned(grad_wdown), owned(grad_wup)
    for c in others:
        norm2(c)
    step.also(*grad_heads[first_clip][1:])
    grad_wout = products(ordered(contexts), grad_branches, half)
    step.mark(grad_wout)
    quarters = arrange(
        scatter_blocks_kernel, [grad_wout],
        [jax.ShapeDtypeStruct((width, -(-span // LANES) * LANES), half)] * groups, groups, me,
        "split_output_weight",
    )
    attention_back(first_clip)
    grad_wout = scatter_terms(lambda r: quarters[r], Order())
    grad_wout = add_terms([step.after(grad_wout[0])] + grad_wout[1:]).astype(half)
    step.mark(grad_wout)
    for c in others:
        attention_back(c)
    step.also(grad_wup)
    total = products(ordered(full1), grad_qkvs, half, beside=grad_wout, width=span)
    step.mark(total)
    total = owned(total)
    for c in every:
        hidden_back(c)
    for c in every:
        norm1_back(c)
    grad_wdown, grad_wup = (gather_all(g) for g in step.after_all([grad_wdown, grad_wup]))
    late = step.after_all(grad_qkvs)
    frames_out = jnp.stack(outs)
    grad_gain1, grad_bias1 = (sum(g) for g in zip(*norm1_grads))
    grad_gain2, grad_bias2 = (sum(g) for g in zip(*norm2_grads))
    grad_dbias = sum(jnp.sum(g.astype(half).astype(single), axis=0) for g in grad_outs)
    grad_ubias = sum(jnp.sum(g.astype(single), axis=0) for blocks in grad_uppers for g in blocks)
    grad_obias = sum(jnp.sum(g.astype(single), axis=0) for g in grad_branches)
    grad_qkv_bias = sum(jnp.sum(g.astype(single), axis=0) for g in late)

    def rows8(v):
        return v.reshape(owners, depth)

    def spread(v):
        return lax.dynamic_update_slice(jnp.zeros((width,), single), v, (me * span,))

    slot = (jnp.arange(groups) == me).astype(single)[None, :, None]
    rows = jnp.concatenate(
        [rows8(grad_gain1), rows8(grad_bias1), rows8(spread(grad_qkv_bias[:span])),
         rows8(spread(grad_qkv_bias[2 * span :])), rows8(grad_obias), rows8(grad_gain2),
         rows8(grad_bias2), rows8(grad_dbias),
         (grad_ubias.reshape(owners, 1, part) * slot).reshape(owners, units)],
        axis=1,
    )
    rows = jnp.take(rows, own ^ jnp.arange(owners), axis=0)
    bits = owners // 2
    while bits:
        rows = rows[:bits] + flip(rows[bits:], bits, "fsdp")
        bits //= 2
    rows = jnp.concatenate([rows[0], jnp.stack(losses)])
    bits = 1
    while bits < groups:
        rows = rows + flip(rows, bits)
        bits *= 2
    step.mark(rows)
    small = [rows[k * depth : (k + 1) * depth] for k in range(8)]
    small_up = rows[8 * depth : 8 * depth + units]
    clip_loss = rows[8 * depth + units :]

    total = step.after(total)
    pieces_last = gather_all(total)
    step.mark(total)
    grad_in = jnp.stack(step.after_all(grads_in))
    grad_wdown = assemble(step.after_all(grad_wdown), 0, me)
    grad_wup = assemble(step.after_all(grad_wup), owners, me)
    step.mark(grad_in, grad_wdown, grad_wup)
    pieces_last = pieces_last[:1] + step.after_all(pieces_last[1:])
    grad_wqkv = assemble(pieces_last, 3, me, 0, 3 * span)
    grad_wout = assemble(pieces_last, 1, me, 3 * span, span)
    return (
        frames_out, clip_loss, grad_in, small[0], small[1], grad_wqkv, small[2], small[3],
        grad_wout, small[4], small[5], small[6], grad_wup, small_up, grad_wdown, small[7],
    )


def solution(mesh):
    vec, mat, act = P("fsdp"), P("fsdp", None), P("fsdp", "seq", None)
    return jax.shard_map(
        local,
        mesh=mesh,
        in_specs=(act, act, P(), vec, vec, mat, vec, vec, mat, vec, vec, vec, mat, vec, mat, vec),
        out_specs=(act, vec, act, vec, vec, mat, vec, vec, mat, vec, vec, vec, mat, vec, mat, vec),
        check_vma=False,
    )
```

```python
import functools
import math

import jax
import jax.numpy as jnp
from jax import lax
from jax.experimental import pallas as pl
from jax.experimental.pallas import tpu as pltpu
from jax.sharding import PartitionSpec as P

HEADS = 16
LANES = 128
LOG2E = 1.0 / math.log(2.0)
single = jnp.float32
half = jnp.bfloat16


def norm_stats(v):
    mean = jnp.mean(v, axis=-1, keepdims=True)
    cent = v - mean
    var = jnp.mean(cent * cent, axis=-1, keepdims=True)
    return mean, lax.rsqrt(var + 1e-05)


def layer_norm(v, stats, gain, bias):
    return (v - stats[0]) * stats[1] * gain + bias


def norm_back(v, stats, gain, grad):
    scaled = (v - stats[0]) * stats[1]
    inner = grad * gain
    first = jnp.mean(inner, axis=-1, keepdims=True)
    second = jnp.mean(inner * scaled, axis=-1, keepdims=True)
    return (
        stats[1] * (inner - first - scaled * second),
        jnp.sum(grad * scaled, axis=0),
        jnp.sum(grad, axis=0),
    )


def flip(tensor, bits, axis="seq"):
    return lax.ppermute(
        tensor, axis, [(i, i ^ bits) for i in range(lax.axis_size(axis))]
    )


def gather_low(piece, size):
    blocks = {0: piece}
    bits = size // 2
    while bits:
        for r in sorted(blocks):
            blocks[r | bits] = flip(blocks[r], bits)
        bits //= 2
    return [blocks[r] for r in range(size)]


def gather_begin(piece):
    size = lax.axis_size("seq") // 2
    far = flip(piece, size)
    return gather_low(piece, size), far


def gather_end(far):
    return gather_low(far, lax.axis_size("seq") // 2)


def gather_all(piece):
    near, far = gather_begin(piece)
    return near + gather_end(far)


def scatter_terms(make, step):
    groups = lax.axis_size("seq")

    def terms(base, size):
        if size == 1:
            out = make(base)
            step.mark(out)
            return [out]
        near = size // 2
        high = terms(base + near, near)
        if len(high) > 1:
            high = step.after(high[0]).astype(single) + sum(h.astype(single) for h in high[1:])
            high = high.astype(half)
            step.mark(high)
        else:
            high = high[0]
        moved = flip(high, near)
        return terms(base, near) + [moved]

    return terms(0, groups)


def add_terms(parts):
    return sum(p.astype(single) for p in parts)


def swap(parts):
    return [parts[0]] + [flip(parts[r], r) for r in range(1, len(parts))]


def pad_lanes(tensor, tail):
    return jnp.concatenate([tensor, tail], axis=1)


def unit_tail(rows, width):
    lane = lax.broadcasted_iota(jnp.int32, (rows, width), 1)
    return jnp.where(lane == 0, 1.0, 0.0).astype(half)


def attend_kernel(heads, dim, block, scale, qkv_ref, mask_ref, ctx_ref, lse_ref, keys, values):
    seq = qkv_ref.shape[0]
    span = heads * dim
    rest = LANES - dim
    rate = scale * LOG2E
    for j in range(heads):
        keys[j] = pad_lanes(
            qkv_ref[:, span + j * dim : span + (j + 1) * dim], mask_ref[...]
        )
        values[j] = pad_lanes(
            qkv_ref[:, 2 * span + j * dim : 2 * span + (j + 1) * dim], unit_tail(seq, rest)
        )

    def one_block(i, carry):
        rows = pl.ds(pl.multiple_of(i * block, block), block)
        ones = unit_tail(block, rest)
        contexts, sums = [], []
        for j in range(heads):
            query = pad_lanes(qkv_ref[rows, j * dim : (j + 1) * dim], ones)
            scores = lax.dot_general(
                query, keys[j], (((1,), (1,)), ((), ())), preferred_element_type=single
            )
            top = jnp.max(scores, axis=-1, keepdims=True) * rate
            probs = jnp.exp2(scores * rate - top).astype(half)
            mixed = jnp.dot(probs, values[j], preferred_element_type=single)
            total = mixed[:, dim : dim + 1]
            contexts.append((mixed[:, :dim] / total).astype(half))
            sums.append(top + jnp.log(total) * LOG2E)
        ctx_ref[rows, :] = jnp.concatenate(contexts, axis=1)
        lse_ref[rows, :] = jnp.concatenate(sums, axis=1)
        return carry

    lax.fori_loop(0, seq // block, one_block, 0)


def attend_back_kernel(
    heads, dim, block, scale,
    qkv_ref, mask_ref, grad_ref, lse_ref, out_ref, keys, values, gkeys, gvalues, gquery,
):
    seq = qkv_ref.shape[0]
    span = heads * dim
    rest = LANES - dim
    rate = scale * LOG2E
    for j in range(heads):
        keys[j] = pad_lanes(
            qkv_ref[:, span + j * dim : span + (j + 1) * dim], mask_ref[...]
        )
        values[j] = pad_lanes(
            qkv_ref[:, 2 * span + j * dim : 2 * span + (j + 1) * dim],
            jnp.zeros((seq, rest), half),
        )
    gkeys[...] = jnp.zeros_like(gkeys)
    gvalues[...] = jnp.zeros_like(gvalues)

    def one_block(i, carry):
        rows = pl.ds(pl.multiple_of(i * block, block), block)
        ones = unit_tail(block, rest)
        none = jnp.zeros((block, rest), half)
        pieces = []
        for j in range(heads):
            query = pad_lanes(qkv_ref[rows, j * dim : (j + 1) * dim], ones)
            grad = pad_lanes(grad_ref[rows, j * dim : (j + 1) * dim], none)
            scores = lax.dot_general(
                query, keys[j], (((1,), (1,)), ((), ())), preferred_element_type=single
            )
            probs = jnp.exp2(scores * rate - lse_ref[rows, j : j + 1])
            dprobs = lax.dot_general(
                grad, values[j], (((1,), (1,)), ((), ())), preferred_element_type=single
            )
            inner = jnp.sum(probs * dprobs, axis=-1, keepdims=True)
            dscores = (probs * (dprobs - inner)).astype(half)
            pieces.append(
                (jnp.dot(dscores, keys[j], preferred_element_type=single)[:, :dim] * scale).astype(half)
            )
            gkeys[j] += jnp.dot(query.T, dscores, preferred_element_type=single)
            gvalues[j] += jnp.dot(grad.T, probs.astype(half), preferred_element_type=single)
        gquery[rows, :] = jnp.concatenate(pieces, axis=1)
        return carry

    lax.fori_loop(0, seq // block, one_block, 0)

    def put(i, carry):
        rows = pl.ds(pl.multiple_of(i * block, block), block)
        pieces = [gquery[rows, :]]
        for j in range(heads):
            pieces.append((gkeys[j, :, rows].T[:, :dim] * scale).astype(half))
        for j in range(heads):
            pieces.append(gvalues[j, :, rows].T[:, :dim].astype(half))
        out_ref[rows, :] = jnp.concatenate(pieces, axis=1)
        return carry

    lax.fori_loop(0, seq // block, put, 0)


def attend(qkv, mask, heads, dim, scale):
    seq = qkv.shape[0]
    block = next(b for b in (768, 512, 256, seq) if seq % b == 0)
    return pl.pallas_call(
        functools.partial(attend_kernel, heads, dim, block, scale),
        out_shape=(
            jax.ShapeDtypeStruct((seq, heads * dim), half),
            jax.ShapeDtypeStruct((seq, heads), single),
        ),
        scratch_shapes=[
            pltpu.VMEM((heads, seq, LANES), half),
            pltpu.VMEM((heads, seq, LANES), half),
        ],
        compiler_params=pltpu.CompilerParams(vmem_limit_bytes=48 << 20),
        cost_estimate=pl.CostEstimate(
            flops=4 * heads * seq * seq * 256, bytes_accessed=qkv.size * 3, transcendentals=heads * seq * seq
        ),
        name="attend",
    )(qkv, mask)


def attend_back(qkv, mask, grad, lse, heads, dim, scale):
    seq = qkv.shape[0]
    block = next(b for b in (768, 512, 256, seq) if seq % b == 0)
    return pl.pallas_call(
        functools.partial(attend_back_kernel, heads, dim, block, scale),
        out_shape=jax.ShapeDtypeStruct(qkv.shape, half),
        scratch_shapes=[
            pltpu.VMEM((heads, seq, LANES), half),
            pltpu.VMEM((heads, seq, LANES), half),
            pltpu.VMEM((heads, LANES, seq), single),
            pltpu.VMEM((heads, LANES, seq), single),
            pltpu.VMEM((seq, heads * dim), half),
        ],
        compiler_params=pltpu.CompilerParams(vmem_limit_bytes=56 << 20),
        cost_estimate=pl.CostEstimate(
            flops=16 * heads * seq * seq * 256, bytes_accessed=qkv.size * 5, transcendentals=heads * seq * seq
        ),
        name="attend_back",
    )(qkv, mask, grad, lse)


def norm_kernel(groups, chunk, *refs):
    blocks, gain_ref, bias_ref, out = refs[:groups], refs[groups], refs[groups + 1], refs[groups + 2]
    rows = blocks[0].shape[0]
    for r in range(groups):

        def some(i, carry, r=r):
            start = pl.multiple_of(i * chunk, chunk)
            v = blocks[r][pl.ds(start, chunk), :].astype(single)
            out[pl.ds(r * rows + start, chunk), :] = layer_norm(v, norm_stats(v), gain_ref[...], bias_ref[...]).astype(
                half
            )
            return carry

        lax.fori_loop(0, rows // chunk, some, 0)


def norm_blocks(blocks, gain, bias):
    groups = len(blocks)
    rows, width = blocks[0].shape
    return pl.pallas_call(
        functools.partial(norm_kernel, groups, 64 if rows % 128 else 128),
        out_shape=jax.ShapeDtypeStruct((groups * rows, width), half),
        cost_estimate=pl.CostEstimate(
            flops=groups * rows * width * 10, bytes_accessed=groups * rows * width * 4, transcendentals=0
        ),
        name="norm_blocks",
    )(*blocks, gain, bias)


def products_kernel(pairs, before, beside, *refs):
    lefts, rights = refs[:pairs], refs[pairs : 2 * pairs]
    more, out = refs[2 * pairs : -1], refs[-1]
    total = more[0][...] if before else None
    for a, b in zip(lefts, rights):
        term = lax.dot_general(
            a[...], b[...], (((0,), (0,)), ((), ())), preferred_element_type=single
        )
        total = term if total is None else total + term
    total = total.astype(out.dtype)
    if beside:
        total = jnp.concatenate([total, more[-1][:, :beside]], axis=1)
    out[...] = total


def products(lefts, rights, kind, before=None, beside=None, width=0, into=None, slot=0, slots=1):
    pairs = len(lefts)
    rows, cols = lefts[0].shape[1], rights[0].shape[1]
    tile = next(t for t in (256, 128, rows) if rows % t == 0)
    depth = sum(a.shape[0] for a in lefts)
    in_specs = [pl.BlockSpec((a.shape[0], tile), lambda i: (0, i)) for a in lefts]
    in_specs += [pl.BlockSpec(b.shape, lambda i: (0, 0)) for b in rights]
    more = []
    if before is not None:
        more.append(before)
        in_specs.append(pl.BlockSpec((tile, cols), lambda i: (i, 0)))
    if beside is not None:
        more.append(beside)
        in_specs.append(pl.BlockSpec((tile, beside.shape[1]), lambda i: (i, 0)))
        cols += width
    body = functools.partial(products_kernel, pairs, before is not None, width)
    aliases = {}
    if into is not None:
        aliases = {2 * pairs + len(more): 0}
        more.append(into)
        in_specs.append(pl.BlockSpec(memory_space=pl.ANY))
        inner = body

        def body(*refs):
            inner(*refs[:-2], refs[-1])

    return pl.pallas_call(
        body,
        grid=(rows // tile,),
        in_specs=in_specs,
        out_specs=pl.BlockSpec((tile, cols), lambda i: (i, slot)),
        out_shape=jax.ShapeDtypeStruct((rows, cols * slots), kind),
        input_output_aliases=aliases,
        compiler_params=pltpu.CompilerParams(vmem_limit_bytes=56 << 20),
        cost_estimate=pl.CostEstimate(
            flops=2 * depth * rows * cols, bytes_accessed=2 * depth * (rows + cols), transcendentals=0
        ),
        name="products",
    )(*lefts, *rights, *more)


def spread_kernel(grad, weight, *outs):
    n = outs[0].shape[0]
    for r, out in enumerate(outs):
        out[...] = lax.dot_general(
            grad[r * n : (r + 1) * n, :], weight[...], (((1,), (1,)), ((), ())),
            preferred_element_type=single,
        ).astype(half)


def spread_terms(grad, weight, groups):
    rows, cols = grad.shape[0] // groups, weight.shape[0]
    return pl.pallas_call(
        spread_kernel,
        out_shape=[jax.ShapeDtypeStruct((rows, cols), half)] * groups,
        compiler_params=pltpu.CompilerParams(vmem_limit_bytes=32 << 20),
        cost_estimate=pl.CostEstimate(flops=0, bytes_accessed=0, transcendentals=0),
        name="spread_terms",
    )(grad, weight)


def assemble_kernel(groups, counts, width, start, me_ref, *refs):
    pieces, out = refs[:groups], refs[groups]
    rows = pieces[0].shape[0]
    for v in range(groups):

        @pl.when(me_ref[0] == v)
        def _():
            for g in range(groups):
                piece = pieces[v ^ g]
                if counts == 0:
                    out[g * rows : (g + 1) * rows, :] = piece[...].astype(single)
            if counts:
                blocks = [
                    pieces[v ^ g][:, start + k * width : start + (k + 1) * width]
                    for k in range(counts)
                    for g in range(groups)
                ]
                out[...] = jnp.concatenate(blocks, axis=1).astype(single)


def assemble(pieces, counts, me, start=0, cols=None):
    groups = len(pieces)
    rows = pieces[0].shape[0]
    cols = cols or pieces[0].shape[1]
    shape = (rows, cols * groups) if counts else (rows * groups, cols)
    return pl.pallas_call(
        functools.partial(assemble_kernel, groups, counts, cols // max(counts, 1), start),
        out_shape=jax.ShapeDtypeStruct(shape, single),
        in_specs=[pl.BlockSpec(memory_space=pltpu.SMEM)]
        + [pl.BlockSpec(memory_space=pltpu.VMEM)] * groups,
        cost_estimate=pl.CostEstimate(
            flops=0, bytes_accessed=rows * cols * groups * 6, transcendentals=0
        ),
        name="assemble",
    )(me.astype(jnp.int32).reshape(1), *pieces)


def gather_blocks_kernel(groups, me_ref, *refs):
    pieces, out = refs[:groups], refs[groups]
    span = pieces[0].shape[1]
    for v in range(groups):

        @pl.when(me_ref[0] == v)
        def _():
            for r in range(groups):
                rows = [
                    pieces[v ^ g][(v ^ r) * span : ((v ^ r) + 1) * span, :] for g in range(groups)
                ]
                out[r * span : (r + 1) * span, :] = jnp.concatenate(rows, axis=1)


def scatter_blocks_kernel(groups, me_ref, full, *outs):
    span = full.shape[1] // groups
    spare = outs[0].shape[1] - span
    for v in range(groups):

        @pl.when(me_ref[0] == v)
        def _():
            for r in range(groups):
                for g in range(groups):
                    block = full[
                        (v ^ g) * span : ((v ^ g) + 1) * span, (v ^ r) * span : ((v ^ r) + 1) * span
                    ]
                    if spare:
                        block = jnp.concatenate([block, jnp.zeros((span, spare), block.dtype)], axis=1)
                    outs[r][g * span : (g + 1) * span, :] = block


def arrange(kernel, arrays, shapes, groups, me, name):
    return pl.pallas_call(
        functools.partial(kernel, groups),
        out_shape=shapes,
        in_specs=[pl.BlockSpec(memory_space=pltpu.SMEM)]
        + [pl.BlockSpec(memory_space=pltpu.VMEM)] * len(arrays),
        cost_estimate=pl.CostEstimate(
            flops=0, bytes_accessed=sum(x.size for x in arrays) * 4, transcendentals=0
        ),
        name=name,
    )(me.astype(jnp.int32).reshape(1), *arrays)


class Order:
    def __init__(self):
        self.tokens = []

    def after(self, tensor):
        if not self.tokens:
            return tensor
        return lax.optimization_barrier((tensor, *self.tokens))[0]

    def after_all(self, tensors):
        return list(lax.optimization_barrier((*tensors, *self.tokens))[: len(tensors)])

    def mark(self, *tensors):
        self.tokens = list(tensors)

    def also(self, *tensors):
        self.tokens += tensors


def local(
    frames_in, teacher, lengths, norm1_gain, norm1_bias, w_qkv, query_bias, value_bias,
    w_attn_out, attn_out_bias, norm2_gain, norm2_bias, w_up, up_bias, w_down, down_bias,
):
    clips, frames, width = frames_in.shape
    groups = lax.axis_size("seq")
    owners = lax.axis_size("fsdp")
    me = lax.axis_index("seq")
    own = lax.axis_index("fsdp")
    seq_len = frames * groups
    dim = width // HEADS
    heads = HEADS // groups
    span = heads * dim
    depth = w_qkv.shape[0]
    units = w_down.shape[0]
    part = units // groups
    scale = 1.0 / math.sqrt(dim)

    def dot(a, b):
        return jnp.dot(a, b, preferred_element_type=single)

    def dot_t(a, b):
        return lax.dot_general(a, b, (((1,), (1,)), ((), ())), preferred_element_type=single)

    def t_dot(a, b):
        return lax.dot_general(a, b, (((0,), (0,)), ((), ())), preferred_element_type=single)

    def columns(array, start, size):
        return lax.dynamic_slice_in_dim(array, start, size, 1)

    def butterfly(array):
        bits = 1
        while bits < owners:
            array = jnp.concatenate([array, flip(array, bits, "fsdp")], axis=0)
            bits *= 2
        return [
            lax.dynamic_index_in_dim(array, own ^ f, 0, keepdims=False) for f in range(owners)
        ]

    ff = owners * part
    first = jnp.concatenate(
        [columns(w_qkv, k * width + me * span, span) for k in range(3)]
        + [columns(w_attn_out, me * span, span)],
        axis=1,
    )
    first = lax.all_gather(first, "fsdp", axis=0, tiled=True)
    wqkv = first[:, : 3 * span]
    wup = jnp.concatenate([columns(w_up, f * units + me * part, part) for f in range(owners)], axis=1)
    wdown = lax.dynamic_slice_in_dim(w_down, me * part, part, 0)
    if part == depth:
        second = lax.all_gather(jnp.concatenate([wup, wdown], axis=1), "fsdp", axis=0, tiled=True)
        wup, wdown = second[:, :ff], second[:, ff:]
    else:
        wup = lax.all_gather(wup, "fsdp", axis=0, tiled=True)
        wdown = lax.all_gather(wdown, "fsdp", axis=0, tiled=True)

    states = []
    for c in range(clips):
        piece = frames_in[c]
        if states:
            piece = lax.optimization_barrier((piece, states[-1][0][-1]))[0]
        states.append(gather_begin(piece))

    packed = jnp.concatenate(
        [norm1_gain, norm1_bias, query_bias, value_bias, attn_out_bias, norm2_gain, norm2_bias,
         down_bias, up_bias]
    )[None]
    vectors = jnp.stack(butterfly(packed)).astype(single)

    def vector(k):
        return vectors[:, k * depth : (k + 1) * depth].reshape(1, width)

    gain1, bias1, qbias, vbias, obias, gain2, bias2, dbias = (vector(k) for k in range(8))
    ubias = lax.dynamic_slice_in_dim(vectors, 8 * depth + me * part, part, 1).reshape(1, ff)
    qkv_bias = jnp.concatenate(
        [columns(qbias, me * span, span), jnp.zeros((1, span), single), columns(vbias, me * span, span)],
        axis=1,
    )

    quarters = gather_all(first[:, 3 * span :])

    mine = lax.dynamic_slice_in_dim(lengths, own * clips, clips)
    order = (me ^ jnp.arange(groups, dtype=jnp.int32))[:, None] * frames + jnp.arange(
        frames, dtype=jnp.int32
    )
    order = order.reshape(seq_len)
    count = jnp.sum(lengths).astype(single)
    lane0 = (jnp.arange(LANES - dim) == 0)[None, :]
    masks = [
        jnp.where((order >= mine[c])[:, None] & lane0, -1e30, 0.0).astype(half) for c in range(clips)
    ]
    row_valid = [(order[:frames] < mine[c]).astype(single)[:, None] for c in range(clips)]

    step = Order()

    n = frames
    every = range(clips)
    full1 = [None] * clips
    qkvs, sums, moved, contexts = ([None] * clips for _ in range(4))
    middles, hiddens, actives, slopes, branches = ([None] * clips for _ in range(5))
    outs, losses, grad_outs, pieces = ([None] * clips for _ in range(4))
    grad_uppers, grad_hidden2, grad_middles, grad_branches = ([None] * clips for _ in range(4))
    grad_heads, grad_qkvs, grad_hidden1, grads_in = ([None] * clips for _ in range(4))
    stats2 = [None] * clips
    norm2_grads, norm1_grads = [None] * clips, [None] * clips

    def rows_of(array, r):
        return array[r * n : (r + 1) * n]

    def owned(grad):
        return lax.psum_scatter(grad, "fsdp", scatter_dimension=0, tiled=True)

    def arriving(store, c):
        near, far = store[c]
        yield from near
        far = gather_end(step.after(far))
        store[c] = near + far
        yield from far

    def norm1(c):
        near, far = states[c]
        full1[c] = norm_blocks(near + gather_end(step.after(far)), gain1, bias1)
        step.mark(full1[c])

    def attention(c):
        qkvs[c] = (dot(step.after(full1[c]), wqkv) + qkv_bias).astype(half)
        context, sums[c] = attend(qkvs[c], masks[c], heads, dim, scale)
        parts = [rows_of(context, r) for r in range(groups)]
        step.mark(*parts)
        moved[c] = swap(parts)

    def project(c):
        contexts[c] = jnp.concatenate(moved[c][:1] + step.after_all(moved[c][1:]), axis=1)
        middles[c] = frames_in[c].astype(single) + dot(contexts[c], wout) + obias
        stats2[c] = norm_stats(middles[c])
        hidden = layer_norm(middles[c], stats2[c], gain2, bias2).astype(half)
        step.mark(hidden)
        hiddens[c] = gather_begin(hidden)

    def feed_forward(c):
        near, far = hiddens[c]
        hiddens[c] = near + gather_end(step.after(far))
        actives[c], slopes[c] = [None] * groups, [None] * groups

        def term(r):
            upper = dot(step.after(hiddens[c][r]), wup) + ubias
            cdf = 0.5 * (1.0 + lax.erf(upper * math.sqrt(0.5)))
            actives[c][r] = (upper * cdf).astype(half)
            slopes[c][r] = (
                cdf + upper * (jnp.exp(-0.5 * upper * upper) * (1.0 / math.sqrt(2.0 * math.pi)))
            ).astype(half)
            step.mark(actives[c][r])
            return marked(dot(step.after(actives[c][r]), wdown).astype(half))

        branches[c] = scatter_terms(term, step)

    def loss(c):
        branch = add_terms(branches[c][:1] + step.after_all(branches[c][1:]))
        result = middles[c] + branch + dbias
        outs[c] = result.astype(half)
        diff = result - teacher[c].astype(single)
        masked = diff * row_valid[c]
        losses[c] = jnp.sum(masked * diff) / (2.0 * width * count)
        grad_outs[c] = masked * (float(lengths.shape[0] * seq_len) / count)
        branch = grad_outs[c].astype(half)
        step.mark(branch)
        pieces[c] = gather_begin(branch)

    def back_up(c):
        grad_uppers[c] = []
        for block in arriving(pieces, c):
            grad = dot_t(step.after(block), wdown) * slopes[c][len(grad_uppers[c])].astype(single)
            grad_uppers[c].append(grad.astype(half))
            step.mark(grad_uppers[c][-1])

    def back_down(c):
        grad_hidden2[c] = scatter_terms(
            lambda r: marked(dot_t(step.after(grad_uppers[c][r]), wup).astype(half)), step
        )

    def norm2(c):
        grad = add_terms(grad_hidden2[c][:1] + step.after_all(grad_hidden2[c][1:]))
        gm, *norm2_grads[c] = norm_back(middles[c], stats2[c], gain2, grad)
        grad_middles[c] = grad_outs[c] + gm
        grad_branches[c] = grad_middles[c].astype(half)
        grad_context = dot_t(grad_branches[c], wout).astype(half)
        parts = [grad_context[:, r * span : (r + 1) * span] for r in range(groups)]
        step.mark(*parts)
        grad_heads[c] = swap(parts)

    def attention_back(c):
        grad_head = jnp.concatenate(grad_heads[c][:1] + step.after_all(grad_heads[c][1:]), axis=0)
        grad_qkvs[c] = attend_back(qkvs[c], masks[c], grad_head, sums[c], heads, dim, scale)
        step.mark(grad_qkvs[c])

    def marked(tensor):
        step.mark(tensor)
        return tensor

    def hidden_back(c):
        found = spread_terms(step.after(grad_qkvs[c]), wqkv, groups)
        step.mark(*found)
        grad_hidden1[c] = scatter_terms(lambda r: found[r], step)

    def norm1_back(c):
        state = frames_in[c].astype(single)
        grad = add_terms(grad_hidden1[c][:1] + step.after_all(grad_hidden1[c][1:]))
        gs, *norm1_grads[c] = norm_back(state, norm_stats(state), gain1, grad)
        grads_in[c] = grad_middles[c] + gs
        step.mark(grads_in[c])

    first_clip, *others = every
    for c in every:
        norm1(c)
    attention(first_clip)
    wout = arrange(
        gather_blocks_kernel, quarters, jax.ShapeDtypeStruct((width, width), half), groups, me,
        "place_output_weight",
    )
    for c in others:
        attention(c)
    for c in every:
        project(c)
    for c in every:
        feed_forward(c)
    for c in every:
        loss(c)
    for c in every:
        back_up(c)
        back_down(c)

    def flat(store):
        return [x for blocks in store for x in blocks]

    def ordered(lefts):
        return [step.after(lefts[0])] + lefts[1:]

    joined = part == depth
    grad_wdown = products(ordered(flat(actives)), flat(pieces), half, slots=1 + joined)
    step.mark(grad_wdown)
    norm2(first_clip)
    grad_wup = products(
        ordered(flat(hiddens)), flat(grad_uppers), half,
        **(dict(into=grad_wdown, slot=1, slots=2) if joined else {}),
    )
    step.mark(grad_wup)
    if joined:
        both = owned(grad_wup)
        grad_wdown, grad_wup = both[:, :width], both[:, width:]
    else:
        grad_wdown, grad_wup = owned(grad_wdown), owned(grad_wup)
    for c in others:
        norm2(c)
    step.also(*grad_heads[first_clip][1:])
    grad_wout = products(ordered(contexts), grad_branches, half)
    step.mark(grad_wout)
    quarters = arrange(
        scatter_blocks_kernel, [grad_wout],
        [jax.ShapeDtypeStruct((width, -(-span // LANES) * LANES), half)] * groups, groups, me,
        "split_output_weight",
    )
    attention_back(first_clip)
    grad_wout = scatter_terms(lambda r: quarters[r], Order())
    grad_wout = add_terms([step.after(grad_wout[0])] + grad_wout[1:]).astype(half)
    step.mark(grad_wout)
    for c in others:
        attention_back(c)
    total = products(ordered(full1), grad_qkvs, half, beside=grad_wout, width=span)
    step.mark(total)
    total = owned(lax.optimization_barrier((total, grad_wup))[0])
    for c in every:
        hidden_back(c)
    for c in every:
        norm1_back(c)
    grad_wdown, grad_wup = (gather_all(g) for g in step.after_all([grad_wdown, grad_wup]))
    late = step.after_all(grad_qkvs)
    frames_out = jnp.stack(outs)
    grad_gain1, grad_bias1 = (sum(g) for g in zip(*norm1_grads))
    grad_gain2, grad_bias2 = (sum(g) for g in zip(*norm2_grads))
    grad_dbias = sum(jnp.sum(g.astype(half).astype(single), axis=0) for g in grad_outs)
    grad_ubias = sum(jnp.sum(g.astype(single), axis=0) for blocks in grad_uppers for g in blocks)
    grad_obias = sum(jnp.sum(g.astype(single), axis=0) for g in grad_branches)
    grad_qkv_bias = sum(jnp.sum(g.astype(single), axis=0) for g in late)

    def rows8(v):
        return v.reshape(owners, depth)

    def spread(v):
        return lax.dynamic_update_slice(jnp.zeros((width,), single), v, (me * span,))

    slot = (jnp.arange(groups) == me).astype(single)[None, :, None]
    rows = jnp.concatenate(
        [rows8(grad_gain1), rows8(grad_bias1), rows8(spread(grad_qkv_bias[:span])),
         rows8(spread(grad_qkv_bias[2 * span :])), rows8(grad_obias), rows8(grad_gain2),
         rows8(grad_bias2), rows8(grad_dbias),
         (grad_ubias.reshape(owners, 1, part) * slot).reshape(owners, units)],
        axis=1,
    )
    rows = jnp.take(rows, own ^ jnp.arange(owners), axis=0)
    bits = owners // 2
    while bits:
        rows = rows[:bits] + flip(rows[bits:], bits, "fsdp")
        bits //= 2
    rows = jnp.concatenate([rows[0], jnp.stack(losses)])
    bits = 1
    while bits < groups:
        rows = rows + flip(rows, bits)
        bits *= 2
    step.mark(rows)
    small = [rows[k * depth : (k + 1) * depth] for k in range(8)]
    small_up = rows[8 * depth : 8 * depth + units]
    clip_loss = rows[8 * depth + units :]

    total = step.after(total)
    pieces_last = gather_all(total)
    step.mark(total)
    grad_in = jnp.stack(step.after_all(grads_in))
    grad_wdown = assemble(step.after_all(grad_wdown), 0, me)
    grad_wup = assemble(step.after_all(grad_wup), owners, me)
    step.mark(grad_in, grad_wdown, grad_wup)
    pieces_last = pieces_last[:1] + step.after_all(pieces_last[1:])
    grad_wqkv = assemble(pieces_last, 3, me, 0, 3 * span)
    grad_wout = assemble(pieces_last, 1, me, 3 * span, span)
    return (
        frames_out, clip_loss, grad_in, small[0], small[1], grad_wqkv, small[2], small[3],
        grad_wout, small[4], small[5], small[6], grad_wup, small_up, grad_wdown, small[7],
    )


def solution(mesh):
    vec, mat, act = P("fsdp"), P("fsdp", None), P("fsdp", "seq", None)
    return jax.shard_map(
        local,
        mesh=mesh,
        in_specs=(act, act, P(), vec, vec, mat, vec, vec, mat, vec, vec, vec, mat, vec, mat, vec),
        out_specs=(act, vec, act, vec, vec, mat, vec, vec, mat, vec, vec, vec, mat, vec, mat, vec),
        check_vma=False,
    )
```
